32 devices in a mesh: shot: 2 (over y), gx: 4 (over z), sec: 2 (over x), gy: 2 (over core).
Axes of the slice: x: 2, y: 2, z: 4, core: 2. Of those that a mesh axis runs over, the one named last changes fastest.
Arguments:
- source_fields: float32 [8, 16, 32, 256], P('shot', 'sec', 'gx', 'gy'), parts along dimension 0, may hold values from -6 to 6
- receiver_fields: float32 [8, 16, 32, 256], P('shot', 'sec', 'gx', 'gy'), parts along dimension 0, may hold values from -6 to 6
- courant: float32 [16, 32, 256], P('sec', 'gx', 'gy'), may hold values from 0.05 to 0.15
- epsilon: float32 [16, 32, 256], P('sec', 'gx', 'gy'), may hold values from 0.05 to 0.3
- delta_param: float32 [16, 32, 256], P('sec', 'gx', 'gy'), may hold values from 0 to 0.15
- tilt_angle: float32 [16, 32, 256], P('sec', 'gx', 'gy'), may hold values from -0.8 to 0.8
- source_pos: int32 [6], P('shot'), parts along dimension 0, may hold values from 0 to 255, as said below
- wavelet: float32 [18], P('shot'), parts along dimension 0, may hold values from -24 to 24
- receiver_pos: int32 [512, 3], P('shot'), parts along dimension 0, may hold values from 0 to 255, as said below
- receiver_data: float32 [18, 256], P('shot'), parts along dimension 0, may hold values from -6 to 6
- step_counts: int32 [3], replicated, may hold values from 1 to 3, as said below
- offset_lags: int32 [48, 2], replicated, may hold values from -8 to 8, as said below
Outputs:
- offset_images: bfloat16 [96, 16, 32, 256], P('shot', 'sec', 'gx', 'gy'), parts along dimension 0
- source_out: float32 [8, 16, 32, 256], P('shot', 'sec', 'gx', 'gy'), parts along dimension 0
- receiver_out: float32 [8, 16, 32, 256], P('shot', 'sec', 'gx', 'gy'), parts along dimension 0
The draws below stay inside these ranges and needn't reach their ends.
There are 2 independent parts, one for each index of `shot`. The reference program is written for one: setup_inputs(seed, part) draws one part's arguments, and reference() takes and returns one part's arrays. A program takes and returns all parts, laid end to end along the dimension named above; an argument that names none is the same for every part. Nothing has to cross between parts.
Inputs may be any that keep to these rules, and one draw needn't show every extreme that they name: `source_pos`: a grid cell: depth below 16, first horizontal below 32, second horizontal below 256; it lies on the last cell of the longest grid dimension and on cell 0 of another dimension. `receiver_pos`: grid cells: depth below 16, first horizontal below 32, second horizontal below 256; one receiver sits at the far corner of the grid and one at its anchor. `step_counts`: some snapshot takes all 3 steps. `offset_lags`: in each dimension some lag is 8 and some is minus 8.
All inputs are finite; a program needn't handle non-finite values.
Results may differ from the reference program's by a relative error of at most 0.001.
The reference program's roundings to bfloat16 on the way count: a program that leaves them out, or rounds other values in their place, can miss the bound.
Values may be sent and summed in bfloat16 or wider, within the bound.
No kernel may reach another device: no remote copies, remote signals or barrier semaphores. Data moves between devices by JAX's collectives and lax.ppermute only.
A program may use at most 64 MiB of HBM per device.

```python
import math
import jax
import jax.numpy as jnp
from jax import lax

SNAPS = 3
STEPS = 3
NLAG = 48
LAG = 8
NREC = 256
NZ = 16
NX = 32
NY = 256
TSLOTS = 9


def draw_cells(key, count):
    keys = jax.random.split(key, 3)
    depth_idx = jax.random.randint(keys[0], (count,), 0, NZ)
    first_idx = jax.random.randint(keys[1], (count,), 0, NX)
    second_idx = jax.random.randint(keys[2], (count,), 0, NY)
    return jnp.stack([depth_idx, first_idx, second_idx], axis=1).astype(jnp.int32)


def draw_source_pos(key, part):
    cell = draw_cells(jax.random.fold_in(key, 11), 1).reshape(3)
    bounds = [NZ, NX, NY]
    longest = 0
    for position in range(3):
        if bounds[position] > bounds[longest]:
            longest = position
    other = (longest + 1) % 3
    slots = lax.iota(jnp.int32, 3)
    cell = jnp.where(slots == longest, bounds[longest] - 1, cell)
    cell = jnp.where(slots == other, 0, cell)
    return cell.astype(jnp.int32)


def draw_receiver_pos(key, part):
    cells = draw_cells(jax.random.fold_in(key, 23), NREC)
    rows = lax.iota(jnp.int32, NREC)[:, None]
    corner = jnp.array([[NZ - 1, NX - 1, NY - 1]], jnp.int32)
    cells = jnp.where(rows == 0, corner, cells)
    cells = jnp.where(rows == 1, 0, cells)
    return cells.astype(jnp.int32)


def draw_step_counts(key, part):
    keys = jax.random.split(jax.random.fold_in(key, 37), 2)
    counts = jax.random.randint(keys[0], (SNAPS,), 1, STEPS + 1)
    chosen = jax.random.randint(keys[1], (), 0, SNAPS)
    return jnp.where(lax.iota(jnp.int32, SNAPS) == chosen, STEPS, counts).astype(jnp.int32)


def draw_offset_lags(key, part):
    keys = jax.random.split(jax.random.fold_in(key, 41), 3)
    values = jax.random.randint(keys[0], (NLAG, 2), -LAG, LAG + 1)
    first_row = jax.random.randint(keys[1], (), 0, NLAG)
    second_row = (first_row + 1 + jax.random.randint(keys[2], (), 0, NLAG - 1)) % NLAG
    rows = lax.iota(jnp.int32, NLAG)[:, None]
    values = jnp.where(rows == first_row, jnp.array([[LAG, -LAG]], jnp.int32), values)
    values = jnp.where(rows == second_row, jnp.array([[-LAG, LAG]], jnp.int32), values)
    return values.astype(jnp.int32)


def block_scale(rng, extent, cuts, smallest, high):
    loudness = 1.0
    for dim, shards_of in cuts:
        steps = jax.random.uniform(jax.random.fold_in(jax.random.fold_in(rng, 6), dim), (shards_of,), jnp.float32, smallest / len(cuts), high / len(cuts))
        loudness = loudness * jnp.repeat(jnp.exp(steps), extent[dim] // shards_of).reshape((-1,) + (1,) * (len(extent) - 1 - dim))
    return loudness


def normal_values(key, shape, deviation, limit, shards=(), kind=jnp.bfloat16):
    drawn = deviation * jax.random.normal(key, shape, jnp.float32)
    if shards:
        drawn = drawn * block_scale(key, shape, shards, -0.22, 0.18)
    return jnp.clip(drawn, -limit, limit).astype(kind)


def setup_inputs(seed: int = 0, part: int = 0) -> dict:
    arg_keys = jax.random.split(jax.random.key(seed), 13)
    part_keys = jax.random.split(jax.random.fold_in(arg_keys[12], part), 13)
    source_fields = normal_values(part_keys[0], (4, NZ, NX, NY), 1.0, 6.0, ((1, 2), (2, 4), (3, 2)), jnp.float32)
    receiver_fields = normal_values(part_keys[1], (4, NZ, NX, NY), 1.0, 6.0, ((1, 2), (2, 4), (3, 2)), jnp.float32)
    courant = jnp.clip(jnp.exp(math.log(0.15) - 1.0986123 * jax.random.uniform(arg_keys[2], (NZ, NX, NY), jnp.float32) ** block_scale(arg_keys[2], (NZ, NX, NY), ((0, 2), (1, 4), (2, 2)), -0.2, 0.2)), 0.05, 0.15)
    epsilon = jnp.clip(0.05 + 0.25 * jax.random.uniform(arg_keys[3], (NZ, NX, NY), jnp.float32) ** block_scale(arg_keys[3], (NZ, NX, NY), ((0, 2), (1, 4), (2, 2)), -0.2, 0.2), 0.05, 0.3)
    delta_param = jnp.clip(0.15 * jax.random.uniform(arg_keys[4], (NZ, NX, NY), jnp.float32) ** block_scale(arg_keys[4], (NZ, NX, NY), ((0, 2), (1, 4), (2, 2)), -0.2, 0.2), 0.0, 0.15)
    tilt_angle = jnp.clip(jax.random.uniform(arg_keys[5], (NZ, NX, NY), jnp.float32, -0.8, 0.8) * block_scale(arg_keys[5], (NZ, NX, NY), ((0, 2), (1, 4), (2, 2)), -0.4, 0.0), -0.8, 0.8)
    source_pos = draw_source_pos(jax.random.fold_in(jax.random.fold_in(arg_keys[12], part), 71), part)
    wavelet = normal_values(part_keys[7], (TSLOTS,), 6.0, 24.0, (), jnp.float32)
    receiver_pos = draw_receiver_pos(jax.random.fold_in(jax.random.fold_in(arg_keys[12], part), 71), part)
    receiver_data = normal_values(part_keys[9], (TSLOTS, NREC), 1.0, 6.0, (), jnp.float32)
    step_counts = draw_step_counts(jax.random.fold_in(arg_keys[12], 71), part)
    offset_lags = draw_offset_lags(jax.random.fold_in(arg_keys[12], 71), part)
    return dict(source_fields=source_fields, receiver_fields=receiver_fields, courant=courant, epsilon=epsilon, delta_param=delta_param, tilt_angle=tilt_angle, source_pos=source_pos, wavelet=wavelet, receiver_pos=receiver_pos, receiver_data=receiver_data, step_counts=step_counts, offset_lags=offset_lags)


def coefficients(courant, epsilon, delta_param, tilt_angle):
    cos_tilt = jnp.cos(tilt_angle)
    sin_tilt = jnp.sin(tilt_angle)
    return (courant, 1.0 + 2.0 * epsilon, 1.0 + 2.0 * delta_param, cos_tilt * cos_tilt, sin_tilt * sin_tilt, 2.0 * sin_tilt * cos_tilt)


def second_diffs(padded):
    center = padded[..., 1:-1, 1:-1, 1:-1]
    along_z = padded[..., 2:, 1:-1, 1:-1] + padded[..., :-2, 1:-1, 1:-1] - 2.0 * center
    along_x = padded[..., 1:-1, 2:, 1:-1] + padded[..., 1:-1, :-2, 1:-1] - 2.0 * center
    along_y = padded[..., 1:-1, 1:-1, 2:] + padded[..., 1:-1, 1:-1, :-2] - 2.0 * center
    cross_xz = 0.25 * (padded[..., 2:, 2:, 1:-1] - padded[..., 2:, :-2, 1:-1] - padded[..., :-2, 2:, 1:-1] + padded[..., :-2, :-2, 1:-1])
    return along_z, along_x, along_y, cross_xz


def advance(padded_p, padded_q, pressure, auxiliary, pressure_old, auxiliary_old, coeffs):
    courant, gain_eps, gain_delta, weight_z, weight_x, weight_mixed = coeffs
    p_zz, p_xx, p_yy, p_xz = second_diffs(padded_p)
    vert_p = weight_z * p_zz + weight_x * p_xx + weight_mixed * p_xz
    horiz_p = p_zz + p_xx + p_yy - vert_p
    q_zz, q_xx, _, q_xz = second_diffs(padded_q)
    vert_q = weight_z * q_zz + weight_x * q_xx + weight_mixed * q_xz
    new_p = 2.0 * pressure - pressure_old + courant * (gain_eps * horiz_p + vert_q)
    new_q = 2.0 * auxiliary - auxiliary_old + courant * (gain_delta * horiz_p + vert_q)
    return new_p, new_q


def deposit(field_3d, points, amounts):
    return field_3d.at[points[:, 0], points[:, 1], points[:, 2]].add(amounts)


def reference(source_fields, receiver_fields, courant, epsilon, delta_param, tilt_angle, source_pos, wavelet, receiver_pos, receiver_data, step_counts, offset_lags):
    coeffs = coefficients(courant, epsilon, delta_param, tilt_angle)
    sections = [[source_fields[member] for member in range(4)], [receiver_fields[member] for member in range(4)]]
    positions = [source_pos.reshape(1, 3), receiver_pos]
    snapshots = []
    for snapshot in range(SNAPS):
        for substep in range(STEPS):
            time_slot = snapshot * STEPS + substep
            active = substep < step_counts[snapshot]
            amounts = [wavelet[time_slot].reshape(1), receiver_data[time_slot]]
            for section in range(2):
                pressure, auxiliary, pressure_old, auxiliary_old = sections[section]
                new_p, new_q = advance(jnp.pad(pressure, 1), jnp.pad(auxiliary, 1), pressure, auxiliary, pressure_old, auxiliary_old, coeffs)
                new_p = deposit(new_p, positions[section], amounts[section])
                new_q = deposit(new_q, positions[section], amounts[section])
                sections[section] = [jnp.where(active, new_p, pressure), jnp.where(active, new_q, auxiliary), jnp.where(active, pressure, pressure_old), jnp.where(active, auxiliary, auxiliary_old)]
        widen = ((0, 0), (LAG, LAG), (LAG, LAG))
        snapshots.append((jnp.pad(sections[0][0].astype(jnp.bfloat16), widen), jnp.pad(sections[1][0].astype(jnp.bfloat16), widen)))

    def image_lag(lag_pair):
        shift_x = lag_pair[0].astype(jnp.int32)
        shift_y = lag_pair[1].astype(jnp.int32)
        start_zero = jnp.zeros((), jnp.int32)
        summed = jnp.zeros((NZ, NX, NY), jnp.float32)
        for source_snap, receiver_snap in snapshots:
            source_win = lax.dynamic_slice(source_snap, (start_zero, (LAG - shift_x).astype(jnp.int32), (LAG - shift_y).astype(jnp.int32)), (NZ, NX, NY))
            receiver_win = lax.dynamic_slice(receiver_snap, (start_zero, (LAG + shift_x).astype(jnp.int32), (LAG + shift_y).astype(jnp.int32)), (NZ, NX, NY))
            summed = summed + source_win.astype(jnp.float32) * receiver_win.astype(jnp.float32)
        return summed

    images = lax.map(image_lag, offset_lags).astype(jnp.bfloat16)
    return images, jnp.stack(sections[0]), jnp.stack(sections[1])
```

```python
import functools

import jax
import jax.numpy as jnp
from jax import lax
from jax.experimental import pallas as pl
from jax.experimental.pallas import tpu as pltpu
from jax.sharding import PartitionSpec as P

SNAPS = 3
STEPS = 3
LAG = 8
HALO = 4
ROWS = 4
WROWS = ROWS + 2 * HALO
ZB = 8
WZ = ZB + 2 * HALO
LANES = 128

F32 = jnp.float32
BF16 = jnp.bfloat16
VM = pl.BlockSpec(memory_space=pltpu.VMEM)
SM = pl.BlockSpec(memory_space=pltpu.SMEM)


def call(body, outs, n_smem, n_vmem, scratch=(), flops=100000, moved=1000000):
    return pl.pallas_call(
        body,
        out_shape=outs,
        in_specs=[SM] * n_smem + [VM] * n_vmem,
        out_specs=[VM] * len(outs),
        scratch_shapes=list(scratch),
        cost_estimate=pl.CostEstimate(flops=flops, bytes_accessed=moved, transcendentals=0),
    )


def half_swap(value):
    return pltpu.roll(value, HALO, 0)


def low_sublanes(shape):
    return lax.broadcasted_iota(jnp.int32, shape, 0) < HALO


def split_body(src, rec, courant, epsilon, delta, tilt, keep, send):
    low = lax.axis_index("gy") == 0

    def put(slot, pick, change=lambda v: v):
        for r in range(ROWS):
            lo = change(pick(pl.ds(r, ZB, stride=2 * ROWS)))
            hi = change(pick(pl.ds(r + ROWS, ZB, stride=2 * ROWS)))
            keep[slot, r] = jnp.where(low, lo, hi)
            send[slot, r] = jnp.where(low, hi, lo)

    for member in range(4):
        put(member, lambda s, m=member: src[m, s, :])
        put(4 + member, lambda s, m=member: rec[m, s, :])
    put(8, lambda s: courant[s, :])
    put(9, lambda s: epsilon[s, :])
    put(10, lambda s: delta[s, :])
    put(11, lambda s: tilt[s, :], jnp.sin)


def edges_of(first, second, sec_size):
    sub = low_sublanes(first.shape)
    top = jnp.where(sub, half_swap(first), second)
    bottom = jnp.where(sub, first, half_swap(second))
    if sec_size == 2:
        return [jnp.where(lax.axis_index("sec") == 0, top, bottom)]
    return [top, bottom]


def merge_body(sec_size, keep, got, own, *edges):
    low = lax.axis_index("gy") == 0

    def pair(j, _):
        for r in range(ROWS):
            both = []
            for k in range(2):
                a, b = keep[2 * j + k, r], got[2 * j + k, r]
                whole = jnp.concatenate([jnp.where(low, a, b), jnp.where(low, b, a)], axis=1)
                own[2 * j + k, r] = whole
                both.append(whole)
            for ref, edge in zip(edges, edges_of(both[0], both[1], sec_size)):
                ref[j, r] = edge
        return 0

    lax.fori_loop(0, 6, pair, 0)


def inject_body(pos, pos_t, data, out):
    x0 = lax.axis_index("gx") * (2 * ROWS) + lax.axis_index("gy") * ROWS - HALO
    z0 = lax.axis_index("sec") * ZB - HALO
    count, side = pos.shape[0], out.shape[3]
    slots = out.shape[0]
    zw = pos_t[0:1, :] - z0
    xw = pos_t[1:2, :] - x0
    inside = (zw >= 0) & (zw < WZ) & (xw >= 0) & (xw < WROWS)
    cell = jnp.where(inside, xw * WZ + zw, -1)
    hit = lax.broadcasted_iota(jnp.int32, (WROWS * WZ, count), 0) == cell
    lanes = lax.broadcasted_iota(jnp.int32, (count, side), 1)
    onehot = jnp.where(lanes == pos[:, 2:3], 1.0, 0.0).astype(BF16)

    for t in range(slots):
        amount = data[t : t + 1, :]
        first = amount.astype(BF16).astype(F32)
        rest = amount - first
        second = rest.astype(BF16).astype(F32)
        third = rest - second
        total = None
        for part in (first, second, third):
            left = jnp.where(hit, part, 0.0).astype(BF16)
            term = jnp.dot(left, onehot, preferred_element_type=F32)
            total = term if total is None else total + term
        out[t] = total.reshape(WROWS, WZ, side)


def assemble(dest, j, base, own, halos, sec_size, slot):
    sec = lax.axis_index("sec")
    for r in range(ROWS):
        sub = low_sublanes(own.shape[2:])
        below = halos[0][j, r]
        if sec_size == 2:
            zero = jnp.zeros_like(below)
            above = jnp.where(sec == 0, below, zero)
            below = jnp.where(sec > 0, below, zero)
        else:
            above = halos[1][j, r]
        lows = (below, half_swap(below))
        highs = (half_swap(above), above)
        for k in range(2):
            mid = half_swap(own[2 * j + k, r])
            ref = dest(slot, k)
            ref[base + r, 0:ZB, :] = jnp.where(sub, lows[k], mid)
            ref[base + r, ZB:WZ, :] = jnp.where(sub, mid, highs[k])


def round_body(number, sec_size, has_snaps, more, last, *refs):
    refs = list(refs)

    def take(n):
        out = refs[:n]
        del refs[:n]
        return out

    nz = 1 if sec_size == 2 else 2
    counts, wavelet, source_pos = take(3)
    groups = []
    for _ in range(3):
        groups.append((take(1)[0], take(nz)))
    coef_groups = []
    for _ in range(3):
        coef_groups.append((take(1)[0], take(nz)))
    inject = take(1)[0]
    snaps_in = take(1)[0] if has_snaps else None
    own_out, snaps = take(2)
    edge_outs = take(nz) if more else []
    final_send = take(1)[0] if last else None
    work, coef, raw = take(3)

    low = lax.axis_index("gy") == 0
    sec = lax.axis_index("sec")
    zero = jnp.int32(0)
    bases = [
        jnp.int32(HALO),
        jnp.where(low, HALO + ROWS, 0),
        jnp.where(low, 0, HALO + ROWS),
    ]

    def fields(j, _):
        for base, (own, halos) in zip(bases, groups):
            assemble(
                lambda slot, k: work.at[j % 2, j // 2, k], j, base, own, halos, sec_size, None
            )
        return 0

    lax.fori_loop(0, 4, fields, 0)

    for j in range(2):
        for base, (own, halos) in zip(bases, coef_groups):
            assemble(lambda slot, k: raw.at[2 * j + k], j, base, own, halos, sec_size, None)

    def derive(x, _):
        c = raw[0, x]
        s = raw[3, x]
        wx = s * s
        wz = 1.0 - wx
        coef[0, x] = c
        coef[1, x] = c * (1.0 + 2.0 * raw[1, x])
        coef[2, x] = c * (1.0 + 2.0 * raw[2, x])
        coef[3, x] = wz
        coef[4, x] = wx
        coef[5, x] = 0.5 * s * jnp.sqrt(wz)
        return 0

    lax.fori_loop(1, WROWS - 1, derive, 0)

    if has_snaps:
        snaps[...] = snaps_in[...]

    ends = []
    total = zero
    for s in range(SNAPS):
        total = total + counts[s]
        ends.append(total)
    first = number * HALO
    todo = jnp.clip(total - first, 0, HALO)
    side = work.shape[-1]
    tile = (WZ, side)
    lane = lax.broadcasted_iota(jnp.int32, tile, 1)
    depth = lax.broadcasted_iota(jnp.int32, tile, 0)
    x0 = lax.axis_index("gx") * (2 * ROWS) + lax.axis_index("gy") * ROWS - HALO
    sx = source_pos[1] - x0
    sz = source_pos[0] - (sec * ZB - HALO)
    sy = source_pos[2]

    def own_cells(parity, section, which, r):
        value = work[parity, section, which, HALO + r]
        sub = low_sublanes((ZB, side))
        return jnp.where(sub, half_swap(value[0:ZB]), half_swap(value[ZB:WZ]))

    def step(j, _):
        active = first + j
        slot = zero
        start = zero
        for s in range(SNAPS):
            slot = jnp.where(active >= start, s * STEPS + active - start, slot)
            start = ends[s]
        cur = j % 2
        new = 1 - cur
        margin = todo - 1 - j

        def row(x, _):
            c, ce, cd, wz, wx, wm = (coef[i, x] for i in range(6))
            for section in range(2):
                p = work[cur, section, 0, x]
                pm = work[cur, section, 0, x - 1]
                pp = work[cur, section, 0, x + 1]
                p2 = 2.0 * p
                diff = pp - pm
                dzz = pltpu.roll(p, 1, 0) + pltpu.roll(p, WZ - 1, 0) - p2
                dxx = pp + pm - p2
                dxz = pltpu.roll(diff, WZ - 1, 0) - pltpu.roll(diff, 1, 0)
                left = jnp.where(lane > 0, pltpu.roll(p, 1, 1), 0.0)
                right = jnp.where(lane < side - 1, pltpu.roll(p, side - 1, 1), 0.0)
                dyy = left + right - p2
                vert = wz * dzz + wx * dxx + wm * dxz
                horiz = dzz + dxx + dyy - vert
                q = work[cur, section, 1, x]
                qm = work[cur, section, 1, x - 1]
                qp = work[cur, section, 1, x + 1]
                q2 = 2.0 * q
                qdiff = qp - qm
                qzz = pltpu.roll(q, 1, 0) + pltpu.roll(q, WZ - 1, 0) - q2
                qxx = qp + qm - q2
                qxz = pltpu.roll(qdiff, WZ - 1, 0) - pltpu.roll(qdiff, 1, 0)
                vq = c * (wz * qzz + wx * qxx + wm * qxz)
                np_ = p2 - work[new, section, 0, x] + (ce * horiz + vq)
                nq_ = q2 - work[new, section, 1, x] + (cd * horiz + vq)
                if section == 1:
                    extra = inject[slot, x]
                    np_ = np_ + extra
                    nq_ = nq_ + extra
                work[new, section, 0, x] = np_
                work[new, section, 1, x] = nq_
            return 0

        lax.fori_loop(HALO - margin, HALO + ROWS + margin, row, 0)

        @pl.when((sx >= 0) & (sx < WROWS))
        def _():
            here = jnp.where((depth == sz) & (lane == sy), wavelet[slot], 0.0)
            for which in range(2):
                work[new, 0, which, sx] = work[new, 0, which, sx] + here

        for s in range(SNAPS):

            @pl.when(active + 1 == ends[s])
            def _():
                for r in range(ROWS):
                    both = [own_cells(new, section, 0, r) for section in range(2)]
                    snaps[s, r] = jnp.concatenate(both, axis=0).astype(BF16)

        return 0

    lax.fori_loop(0, todo, step, 0)

    at = todo % 2
    for section in range(2):
        for old in range(2):
            parity = at if old == 0 else 1 - at
            for r in range(ROWS):
                both = []
                for which in range(2):
                    value = own_cells(parity, section, which, r)
                    member = section * 4 + old * 2 + which
                    own_out[member, r] = value
                    if last:
                        final_send[member, r] = jnp.where(
                            low, value[:, side // 2 :], value[:, : side // 2]
                        )
                    both.append(value)
                if more:
                    for ref, edge in zip(edge_outs, edges_of(both[0], both[1], sec_size)):
                        ref[section * 2 + old, r] = edge


def image_body(lags, own, got, snaps, sib, near, far, sib_near, sib_far, images, src, rec, ext, flip):
    core = lax.axis_index("gy")
    low = core == 0
    half = images.shape[3]
    mine = jnp.where(low, 0, ROWS)
    other = jnp.where(low, ROWS, 0)
    for member in range(8):
        dest = src if member < 4 else rec
        base = (member % 4) * ZB * 2 * ROWS
        for r in range(ROWS):
            value = own[member, r]
            value = jnp.where(low, value[:, :half], value[:, half:])
            dest[pl.ds(base + mine + r, ZB, stride=2 * ROWS), :] = value
            dest[pl.ds(base + other + r, ZB, stride=2 * ROWS), :] = got[member, r]

    lane = lax.broadcasted_iota(jnp.int32, (ZB, half), 1)
    edge = jnp.where(low, 0, half - LAG)
    keep = (lane >= edge) & (lane < edge + LAG)
    pieces = (
        (near, jnp.where(low, ROWS, 4 * ROWS)),
        (far, jnp.where(low, 0, 5 * ROWS)),
        (snaps, jnp.where(low, 2 * ROWS, 3 * ROWS)),
        (sib, jnp.where(low, 3 * ROWS, 2 * ROWS)),
        (sib_near, jnp.where(low, 4 * ROWS, ROWS)),
        (sib_far, jnp.where(low, 5 * ROWS, 0)),
    )
    for piece, base in pieces:
        for s in range(SNAPS):
            for r in range(ROWS):
                value = piece[s, r].astype(F32)
                for section in range(2):
                    cells = value[section * ZB : (section + 1) * ZB]
                    a, b = cells[:, :half], cells[:, half:]
                    ext[s, section, base + r, 0] = jnp.where(low, a, b)
                    ext[s, section, base + r, 1] = jnp.where(keep, jnp.where(low, b, a), 0.0)

    def one_lag(l, _):
        lx = lags[l, 0]
        ly = lags[l, 1]
        s_shift = lax.rem(ly + half, half)
        r_shift = lax.rem(half - ly, half)
        s_own = (lane - ly >= 0) & (lane - ly < half)
        r_own = (lane + ly >= 0) & (lane + ly < half)
        for x in range(2 * ROWS):
            total = None
            for s in range(SNAPS):
                xs = 2 * ROWS + x - lx
                xr = 2 * ROWS + x + lx
                a = jnp.where(
                    s_own,
                    pltpu.roll(ext[s, 0, xs, 0], s_shift, 1),
                    pltpu.roll(ext[s, 0, xs, 1], s_shift, 1),
                )
                b = jnp.where(
                    r_own,
                    pltpu.roll(ext[s, 1, xr, 0], r_shift, 1),
                    pltpu.roll(ext[s, 1, xr, 1], r_shift, 1),
                )
                total = a * b if total is None else total + a * b
            flip[pl.ds(x, ZB, stride=2 * ROWS), :] = total
        for z in range(ZB):
            images[l, z] = flip[z * 2 * ROWS : (z + 1) * 2 * ROWS, :].astype(BF16)
        return 0

    lax.fori_loop(0, lags.shape[0], one_lag, 0)


def local(
    source_fields,
    receiver_fields,
    courant,
    epsilon,
    delta_param,
    tilt_angle,
    source_pos,
    wavelet,
    receiver_pos,
    receiver_data,
    step_counts,
    offset_lags,
):
    sec_size = lax.axis_size("sec")
    gx_size = lax.axis_size("gx")
    depth_cells, wide_cells, half = courant.shape
    side = 2 * half
    sib_pairs = [(0, 1), (1, 0)]
    partner_pairs = []
    for i in range(gx_size - 1):
        partner_pairs += [(2 * i + 1, 2 * i + 2), (2 * i + 2, 2 * i + 1)]

    def sibling(x):
        return lax.ppermute(x, "gy", sib_pairs)

    def partner(x):
        return lax.ppermute(x, ("gx", "gy"), partner_pairs)

    def depth_halos(edges):
        if sec_size == 2:
            return [lax.ppermute(edges[0], "sec", sib_pairs)]
        up = [(i, i + 1) for i in range(sec_size - 1)]
        down = [(i + 1, i) for i in range(sec_size - 1)]
        return [lax.ppermute(edges[0], "sec", up), lax.ppermute(edges[1], "sec", down)]

    def flat(x):
        return x.reshape(x.shape[:-3] + (depth_cells * wide_cells, half))

    part = jax.ShapeDtypeStruct((12, ROWS, ZB, half), F32)
    keep, send = call(split_body, [part, part], 0, 6)(
        flat(source_fields),
        flat(receiver_fields),
        flat(courant),
        flat(epsilon),
        flat(delta_param),
        flat(tilt_angle),
    )
    got = sibling(send)
    nz = 1 if sec_size == 2 else 2
    edge12 = jax.ShapeDtypeStruct((6, ROWS, ZB, side), F32)
    edge8 = jax.ShapeDtypeStruct((4, ROWS, ZB, side), F32)
    merged = call(
        functools.partial(merge_body, sec_size),
        [jax.ShapeDtypeStruct((12, ROWS, ZB, side), F32)] + [edge12] * nz,
        0,
        2,
    )(keep, got)
    own, edges = merged[0], merged[1:]

    slots = receiver_data.shape[0]
    (inject,) = call(
        inject_body, [jax.ShapeDtypeStruct((slots, WROWS, WZ, side), F32)], 0, 3
    )(receiver_pos, receiver_pos.T, receiver_data)

    def exchange(own, edges):
        sib_own, par_own = sibling(own), partner(own)
        halos = depth_halos(edges)
        groups = [(own, halos)]
        groups.append((sib_own, [sibling(h) for h in halos]))
        groups.append((par_own, [partner(h) for h in halos]))
        return groups

    snap_type = jax.ShapeDtypeStruct((SNAPS, ROWS, 2 * ZB, side), BF16)
    own_type = jax.ShapeDtypeStruct((8, ROWS, ZB, side), F32)
    fin_type = jax.ShapeDtypeStruct((8, ROWS, ZB, half), F32)

    def whole_or_part(shape, first, count):
        return pl.BlockSpec((count,) + shape[1:], lambda i, b=first // count: (b, 0, 0, 0))

    def run_round(number, groups, coef_groups, snaps, more, last):
        args, specs = [step_counts, wavelet, source_pos], [SM] * 3
        for own_, halos in groups:
            args.append(own_)
            specs.append(whole_or_part(own_.shape, 0, 8) if own_.shape[0] == 8 else pl.BlockSpec((8,) + own_.shape[1:], lambda i: (0, 0, 0, 0)))
            for h in halos:
                args.append(h)
                specs.append(pl.BlockSpec((4,) + h.shape[1:], lambda i: (0, 0, 0, 0)))
        for own_, halos in coef_groups:
            args.append(own_)
            specs.append(pl.BlockSpec((4,) + own_.shape[1:], lambda i: (2, 0, 0, 0)))
            for h in halos:
                args.append(h)
                specs.append(pl.BlockSpec((2,) + h.shape[1:], lambda i: (2, 0, 0, 0)))
        args.append(inject)
        specs.append(VM)
        if snaps is not None:
            args.append(snaps)
            specs.append(VM)
        outs = [own_type, snap_type]
        if more:
            outs += [edge8] * nz
        if last:
            outs += [fin_type]
        return pl.pallas_call(
            functools.partial(round_body, number, sec_size, snaps is not None, more, last),
            out_shape=outs,
            grid=(1,),
            in_specs=specs,
            out_specs=[VM] * len(outs),
            scratch_shapes=[
                pltpu.VMEM((2, 2, 2, WROWS, WZ, side), F32),
                pltpu.VMEM((6, WROWS, WZ, side), F32),
                pltpu.VMEM((4, WROWS, WZ, side), F32),
            ],
            cost_estimate=pl.CostEstimate(flops=10000000, bytes_accessed=3000000, transcendentals=0),
        )(*args)

    groups0 = exchange(own, edges)
    own, snaps, *edges = run_round(0, groups0, groups0, None, True, False)
    groups = exchange(own, edges)
    own, snaps, *rest = run_round(1, groups, groups0, snaps, True, True)
    edges, final_send = rest[:nz], rest[nz]

    def finish(own, snaps, final_send):
        final_got = sibling(final_send)
        sib = sibling(snaps)
        near, far = partner(snaps), partner(sib)
        sib_near, sib_far = sibling(near), sibling(far)
        n_lags = offset_lags.shape[0]
        out = jax.ShapeDtypeStruct((4 * depth_cells * wide_cells, half), F32)
        images, src, rec = call(
            image_body,
            [jax.ShapeDtypeStruct((n_lags, depth_cells, wide_cells, half), BF16), out, out],
            1,
            8,
            [
                pltpu.VMEM((SNAPS, 2, 6 * ROWS, 2, ZB, half), F32),
                pltpu.VMEM((ZB * 2 * ROWS, half), F32),
            ],
        )(offset_lags, own, final_got, snaps, sib, near, far, sib_near, sib_far)
        shape = (4, depth_cells, wide_cells, half)
        return images, src.reshape(shape), rec.reshape(shape)

    def third(own, snaps, final_send, *edges):
        groups = exchange(own, list(edges))
        own, snaps, final_send = run_round(2, groups, groups0, snaps, False, True)
        return finish(own, snaps, final_send)

    def done(own, snaps, final_send, *edges):
        return finish(own, snaps, final_send)

    return lax.cond(
        jnp.sum(step_counts) > 2 * HALO, third, done, own, snaps, final_send, *edges
    )


def solution(mesh):
    placed = (
        P("shot", "sec", "gx", "gy"),
        P("shot", "sec", "gx", "gy"),
        P("sec", "gx", "gy"),
        P("sec", "gx", "gy"),
        P("sec", "gx", "gy"),
        P("sec", "gx", "gy"),
        P("shot"),
        P("shot"),
        P("shot", None),
        P("shot", None),
        P(),
        P(),
    )
    return jax.shard_map(
        local,
        mesh=mesh,
        in_specs=placed,
        out_specs=(
            P("shot", "sec", "gx", "gy"),
            P("shot", "sec", "gx", "gy"),
            P("shot", "sec", "gx", "gy"),
        ),
        check_vma=False,
    )
```

```python
import functools

import jax
import jax.numpy as jnp
from jax import lax
from jax.experimental import pallas as pl
from jax.experimental.pallas import tpu as pltpu
from jax.sharding import PartitionSpec as P

SNAPS = 3
STEPS = 3
LAG = 8
HALO = 4
ROWS = 4
WROWS = ROWS + 2 * HALO
ZB = 8
WZ = ZB + 2 * HALO
LANES = 128

ROUND_FLAGS = None
F32 = jnp.float32
BF16 = jnp.bfloat16
VM = pl.BlockSpec(memory_space=pltpu.VMEM)
SM = pl.BlockSpec(memory_space=pltpu.SMEM)


def call(body, outs, n_smem, n_vmem, scratch=(), flops=100000, moved=1000000, mib=12, flags=None):
    return pl.pallas_call(
        body,
        out_shape=outs,
        in_specs=[SM] * n_smem + [VM] * n_vmem,
        out_specs=[VM] * len(outs),
        scratch_shapes=list(scratch),
        cost_estimate=pl.CostEstimate(flops=flops, bytes_accessed=moved, transcendentals=0),
        compiler_params=pltpu.CompilerParams(vmem_limit_bytes=mib * 2**20, flags=flags),
    )


def half_swap(value):
    return pltpu.roll(value, HALO, 0)


def low_sublanes(shape):
    return lax.broadcasted_iota(jnp.int32, shape, 0) < HALO


def split_body(src, rec, courant, epsilon, delta, tilt, keep, send):
    low = lax.axis_index("gy") == 0

    def put(slot, pick, change=lambda v: v):
        for r in range(ROWS):
            lo = change(pick(pl.ds(r, ZB, stride=2 * ROWS)))
            hi = change(pick(pl.ds(r + ROWS, ZB, stride=2 * ROWS)))
            keep[slot, r] = jnp.where(low, lo, hi)
            send[slot, r] = jnp.where(low, hi, lo)

    for member in range(4):
        put(member, lambda s, m=member: src[m, s, :])
        put(4 + member, lambda s, m=member: rec[m, s, :])
    put(8, lambda s: courant[s, :])
    put(9, lambda s: epsilon[s, :])
    put(10, lambda s: delta[s, :])
    put(11, lambda s: tilt[s, :], jnp.sin)


def edges_of(first, second, sec_size):
    sub = low_sublanes(first.shape)
    top = jnp.where(sub, half_swap(first), second)
    bottom = jnp.where(sub, first, half_swap(second))
    if sec_size == 2:
        return [jnp.where(lax.axis_index("sec") == 0, top, bottom)]
    return [top, bottom]


def merge_body(sec_size, keep, got, own, *edges):
    low = lax.axis_index("gy") == 0

    def pair(j, _):
        for r in range(ROWS):
            both = []
            for k in range(2):
                a, b = keep[2 * j + k, r], got[2 * j + k, r]
                whole = jnp.concatenate([jnp.where(low, a, b), jnp.where(low, b, a)], axis=1)
                own[2 * j + k, r] = whole
                both.append(whole)
            for ref, edge in zip(edges, edges_of(both[0], both[1], sec_size)):
                ref[j, r] = edge
        return 0

    lax.fori_loop(0, 6, pair, 0)


def inject_body(pos_t, data, out):
    x0 = lax.axis_index("gx") * (2 * ROWS) + lax.axis_index("gy") * ROWS - HALO
    z0 = lax.axis_index("sec") * ZB - HALO
    count, side = pos_t.shape[1], out.shape[3]
    slots = out.shape[0]
    zw = pos_t[0:1, :] - z0
    xw = pos_t[1:2, :] - x0
    inside = (zw >= 0) & (zw < WZ) & (xw >= 0) & (xw < WROWS)
    cell = jnp.where(inside, xw * WZ + zw, -1)
    hit = lax.broadcasted_iota(jnp.int32, (WROWS * WZ, count), 0) == cell
    columns = lax.broadcasted_iota(jnp.int32, (side, count), 0)
    onehot = jnp.where(columns == pos_t[2:3, :], 1.0, 0.0).astype(BF16)

    for t in range(slots):
        amount = data[t : t + 1, :]
        first = amount.astype(BF16).astype(F32)
        rest = amount - first
        second = rest.astype(BF16).astype(F32)
        third = rest - second
        total = None
        for part in (first, second, third):
            left = jnp.where(hit, part, 0.0).astype(BF16)
            term = lax.dot_general(
                left, onehot, (((1,), (1,)), ((), ())), preferred_element_type=F32
            )
            total = term if total is None else total + term
        out[t] = total.reshape(WROWS, WZ, side)


def assemble(dest, j, base, own, halos, here, padded=False):
    sec = lax.axis_index("sec")
    zero = jnp.zeros(own.shape[2:], F32)
    has_low = here & (sec > 0)
    has_high = here & (sec < lax.axis_size("sec") - 1)
    for r in range(ROWS):
        sub = low_sublanes(own.shape[2:])
        below = jnp.where(has_low, halos[0][j, r], zero)
        above = jnp.where(has_high, halos[-1][j, r], zero)
        lows = (below, half_swap(below))
        highs = (half_swap(above), above)
        for k in range(2):
            mid = half_swap(jnp.where(here, own[2 * j + k, r], zero))
            ref = dest(k)
            upper = jnp.where(sub, lows[k], mid)
            lower = jnp.where(sub, mid, highs[k])
            if padded:
                for h in range(own.shape[3] // LANES):
                    lanes = slice(h * LANES, (h + 1) * LANES)
                    ref[base + r, h, ZB : 2 * ZB, :] = upper[:, lanes]
                    ref[base + r, h, 2 * ZB : 3 * ZB, :] = lower[:, lanes]
            else:
                ref[base + r, 0:ZB, :] = upper
                ref[base + r, ZB:WZ, :] = lower


def round_body(number, sec_size, more, last, *refs):
    refs = list(refs)

    def take(n):
        out = refs[:n]
        del refs[:n]
        return out

    opening = number == 0
    nz = 1 if sec_size == 2 else 2
    counts, wavelet, source_pos = take(3)
    groups = [(take(1)[0], take(nz)) for _ in range(3)]
    if not opening:
        coef = take(1)[0]
    inject = take(1)[0]
    snaps_in = None if opening else take(1)[0]
    own_out, snaps = take(2)
    edge_outs = take(nz) if more else []
    final_send = take(1)[0] if last else None
    if opening:
        coef = take(1)[0]
    works = take(2)

    low = lax.axis_index("gy") == 0
    gx = lax.axis_index("gx")
    sec = lax.axis_index("sec")
    zero = jnp.int32(0)
    always = gx >= 0
    has_partner = jnp.where(low, gx, lax.axis_size("gx") - 1 - gx) > 0
    bases = [
        (jnp.int32(HALO), always),
        (jnp.where(low, HALO + ROWS, 0), always),
        (jnp.where(low, 0, HALO + ROWS), has_partner),
    ]

    def fields(i, _):
        for parity in range(2):
            for (base, here), (own, halos) in zip(bases, groups):
                put_at = lambda k, work=works[parity]: work.at[i, k]
                assemble(put_at, 2 * i + parity, base, own, halos, here, True)
        return 0

    lax.fori_loop(0, 2, fields, 0)

    if opening:
        for j in range(2):
            for (base, here), (own, halos) in zip(bases, groups):
                assemble(lambda k: coef.at[2 * j + k], 4 + j, base, own, halos, here)

        def derive(x, _):
            c = coef[0, x]
            s = coef[3, x]
            wx = s * s
            coef[1, x] = c * (1.0 + 2.0 * coef[1, x])
            coef[2, x] = c * (1.0 + 2.0 * coef[2, x])
            coef[3, x] = wx
            coef[4, x] = 0.5 * s * jnp.sqrt(1.0 - wx)
            return 0

        lax.fori_loop(1, WROWS - 1, derive, 0)
    else:
        snaps[...] = snaps_in[...]

    ends = []
    total = zero
    for s in range(SNAPS):
        total = total + counts[s]
        ends.append(total)
    first = number * HALO
    todo = jnp.clip(total - first, 0, HALO)
    n_lane = works[0].shape[3]
    side = n_lane * LANES
    n_depth = WZ // ZB
    v_sub = lax.broadcasted_iota(jnp.int32, (ZB, LANES), 0)
    v_lane = lax.broadcasted_iota(jnp.int32, (ZB, LANES), 1)
    keys = [(t, h) for t in range(n_depth) for h in range(n_lane)]
    x0 = gx * (2 * ROWS) + lax.axis_index("gy") * ROWS - HALO
    sx = source_pos[1] - x0
    sz = source_pos[0] - (sec * ZB - HALO)
    sy = source_pos[2]

    def own_cells(parity, section, which, r):
        start = ZB + HALO
        parts = [
            works[parity][section, which, HALO + r, h, start : start + ZB, :]
            for h in range(n_lane)
        ]
        return jnp.concatenate(parts, axis=1)

    def tiles(ref, *at):
        return {
            (t, h): ref[at + (slice(t * ZB, (t + 1) * ZB), slice(h * LANES, (h + 1) * LANES))]
            for t, h in keys
        }

    def cells(parity, section, which, x, shift=0):
        start = ZB + shift
        return {
            (t, h): works[parity][section, which, x, h, start + t * ZB : start + (t + 1) * ZB, :]
            for t, h in keys
        }

    def side_sum(v):
        left = {k: pltpu.roll(v[k], 1, 1) for k in keys}
        right = {k: pltpu.roll(v[k], LANES - 1, 1) for k in keys}
        out = {}
        for t, h in keys:
            a = jnp.where(v_lane == 0, left.get((t, h - 1), 0.0), left[t, h])
            b = jnp.where(v_lane == LANES - 1, right.get((t, h + 1), 0.0), right[t, h])
            out[t, h] = a + b
        return out

    def put(value, parity, section, which, x):
        for t, h in keys:
            works[parity][section, which, x, h, (t + 1) * ZB : (t + 2) * ZB, :] = value[t, h]

    def step(j):
        active = first + j
        slot = zero
        start = zero
        for s in range(SNAPS):
            slot = jnp.where(active >= start, s * STEPS + active - start, slot)
            start = ends[s]
        cur = j % 2
        new = 1 - cur
        margin = todo - 1 - j

        def one_row(x, c, ce, cd, wx, wm, section):
            p, pm, pp = (cells(cur, section, 0, x + d) for d in (0, -1, 1))
            q, qm, qp = (cells(cur, section, 1, x + d) for d in (0, -1, 1))
            pu, pmu, ppu = (cells(cur, section, 0, x + d, 1) for d in (0, -1, 1))
            pd, pmd, ppd = (cells(cur, section, 0, x + d, -1) for d in (0, -1, 1))
            qu, qmu, qpu = (cells(cur, section, 1, x + d, 1) for d in (0, -1, 1))
            qd, qmd, qpd = (cells(cur, section, 1, x + d, -1) for d in (0, -1, 1))
            ys = side_sum(p)
            po = cells(new, section, 0, x)
            qo = cells(new, section, 1, x)
            extra = tiles(inject, slot, x) if section == 1 else None
            new_p, new_q = {}, {}
            for k in keys:
                zz = pu[k] + pd[k]
                xx = pp[k] + pm[k]
                xz = (ppu[k] - pmu[k]) - (ppd[k] - pmd[k])
                horiz = (xx + ys[k] - 4.0 * p[k]) + wx[k] * (zz - xx) - wm[k] * xz
                q2 = 2.0 * q[k]
                qz = qu[k] + qd[k]
                qx = qp[k] + qm[k]
                qxz = (qpu[k] - qmu[k]) - (qpd[k] - qmd[k])
                vert = c[k] * ((qz - q2) + wx[k] * (qx - qz) + wm[k] * qxz)
                new_p[k] = (2.0 * p[k] - po[k]) + (ce[k] * horiz + vert)
                new_q[k] = (q2 - qo[k]) + (cd[k] * horiz + vert)
                if extra is not None:
                    new_p[k] = new_p[k] + extra[k]
                    new_q[k] = new_q[k] + extra[k]
            put(new_p, new, section, 0, x)
            put(new_q, new, section, 1, x)

        def rows(i, _):
            for u in range(2):
                x = HALO - margin + 2 * i + u
                weights = [tiles(coef, n, x) for n in range(5)]
                for section in range(2):
                    one_row(x, *weights, section)
            return 0

        lax.fori_loop(0, ROWS // 2 + margin, rows, 0)

        @pl.when((sx >= 0) & (sx < WROWS))
        def _():
            amount = wavelet[slot]
            for t, h in keys:
                hit = (v_sub == sz - t * ZB) & (v_lane == sy - h * LANES)
                here = jnp.where(hit, amount, 0.0)
                for which in range(2):
                    at = (0, which, sx, h, slice((t + 1) * ZB, (t + 2) * ZB))
                    works[new][at] = works[new][at] + here

        for s in range(SNAPS):

            @pl.when(active + 1 == ends[s])
            def _():
                for r in range(ROWS):
                    both = [own_cells(new, section, 0, r) for section in range(2)]
                    snaps[s, r] = jnp.concatenate(both, axis=0).astype(BF16)

    for j in range(HALO):
        pl.when(j < todo)(functools.partial(step, j))

    odd = todo % 2 == 1
    for section in range(2):
        for old in range(2):
            for r in range(ROWS):
                both = []
                for which in range(2):
                    value = jnp.where(
                        odd,
                        own_cells(1 - old, section, which, r),
                        own_cells(old, section, which, r),
                    )
                    member = section * 4 + old * 2 + which
                    own_out[member, r] = value
                    if last:
                        final_send[member, r] = jnp.where(
                            low, value[:, side // 2 :], value[:, : side // 2]
                        )
                    both.append(value)
                if more:
                    for ref, edge in zip(edge_outs, edges_of(both[0], both[1], sec_size)):
                        ref[section * 2 + old, r] = edge


def image_body(lags, own, got, snaps, sib, near, far, sib_near, sib_far, images, src, rec, rows, table, flip):
    core = lax.axis_index("gy")
    gx = lax.axis_index("gx")
    low = core == 0
    half = images.shape[3]
    side = rows.shape[-1]
    span = 6 * ROWS
    mine = jnp.where(low, 0, ROWS)
    other = jnp.where(low, ROWS, 0)
    for member in range(8):
        dest = src if member < 4 else rec
        base = (member % 4) * ZB * 2 * ROWS
        for r in range(ROWS):
            value = own[member, r]
            value = jnp.where(low, value[:, :half], value[:, half:])
            dest[pl.ds(base + mine + r, ZB, stride=2 * ROWS), :] = value
            dest[pl.ds(base + other + r, ZB, stride=2 * ROWS), :] = got[member, r]

    left = gx > 0
    right = gx < lax.axis_size("gx") - 1
    mine_on = jnp.where(low, gx, lax.axis_size("gx") - 1 - gx) > 0
    sib_on = jnp.where(low, lax.axis_size("gx") - 1 - gx, gx) > 0
    pieces = (
        (near, jnp.where(low, ROWS, 4 * ROWS), mine_on),
        (far, jnp.where(low, 0, 5 * ROWS), mine_on),
        (snaps, jnp.where(low, 2 * ROWS, 3 * ROWS), None),
        (sib, jnp.where(low, 3 * ROWS, 2 * ROWS), None),
        (sib_near, jnp.where(low, 4 * ROWS, ROWS), sib_on),
        (sib_far, jnp.where(low, 5 * ROWS, 0), sib_on),
    )
    for piece, base, here in pieces:
        for s in range(SNAPS):
            for r in range(ROWS):
                value = piece[s, r]
                if here is not None:
                    value = jnp.where(here, value, jnp.zeros_like(value))
                rows[s * span + base + r] = value

    cells = rows[...].reshape(SNAPS * span * 2 * ZB, side)
    lane = lax.broadcasted_iota(jnp.int32, (side, 2 * half), 1)
    second = (lane >= half).astype(jnp.int32)
    gap = lax.broadcasted_iota(jnp.int32, (side, 2 * half), 0) - core * half - lane + second * (half + 1)

    def shifts(m, _):
        pick = jnp.where(gap == LAG - 2 * m, 1.0, 0.0).astype(BF16)
        moved = jnp.dot(cells, pick, preferred_element_type=F32)
        for h in range(2):
            part = moved[:, h * half : (h + 1) * half]
            table[2 * m + h] = part.reshape(SNAPS * span, 2 * ZB, half)
        return 0

    lax.fori_loop(0, LAG + 1, shifts, 0)

    count = lags.shape[1]
    group = next(g for g in (4, 3, 2, 1) if count % g == 0)

    def some_lags(i, _):
        for u in range(group):
            l = i * group + u
            lx = lags[0, l]
            ly = lags[1, l]
            for x in range(2 * ROWS):
                total = None
                for s in range(SNAPS):
                    at = s * span + 2 * ROWS + x
                    term = table[LAG + ly, at - lx, 0:ZB] * table[LAG - ly, at + lx, ZB : 2 * ZB]
                    total = term if total is None else total + term
                flip[u, pl.ds(x, ZB, stride=2 * ROWS), :] = total
            for z in range(ZB):
                images[l, z] = flip[u, z * 2 * ROWS : (z + 1) * 2 * ROWS, :].astype(BF16)
        return 0

    lax.fori_loop(0, count // group, some_lags, 0)


def local(
    source_fields,
    receiver_fields,
    courant,
    epsilon,
    delta_param,
    tilt_angle,
    source_pos,
    wavelet,
    receiver_pos,
    receiver_data,
    step_counts,
    offset_lags,
):
    sec_size = lax.axis_size("sec")
    gx_size = lax.axis_size("gx")
    depth_cells, wide_cells, half = courant.shape
    side = 2 * half
    shots, nz = lax.axis_size("shot"), (1 if sec_size == 2 else 2)
    axes = ("shot", "gx", "sec", "gy")

    def permute(x, move):
        def rank(d):
            return ((d[0] * gx_size + d[1]) * sec_size + d[2]) * 2 + d[3]

        pairs = [
            (rank((n, g, s, c)), rank(move(n, g, s, c)))
            for n in range(shots)
            for g in range(gx_size)
            for s in range(sec_size)
            for c in range(2)
        ]
        return lax.ppermute(x, axes, pairs)

    def sibling(x):
        return permute(x, lambda n, g, s, c: (n, g, s, 1 - c))

    def facing(n, g, s, c):
        other = g - 1 if c == 0 else g + 1
        if 0 <= other < gx_size:
            return (n, other, s, 1 - c)
        return ((n + 1) % shots, g, s, c)

    def partner(x):
        return permute(x, facing)

    def depth_halos(edges):
        ups = [permute(edges[0], lambda n, g, s, c: (n, g, (s + 1) % sec_size, c))]
        if nz == 2:
            ups.append(permute(edges[1], lambda n, g, s, c: (n, g, (s - 1) % sec_size, c)))
        return ups

    def flat(x):
        return x.reshape(x.shape[:-3] + (depth_cells * wide_cells, half))

    part = jax.ShapeDtypeStruct((12, ROWS, ZB, half), F32)
    keep, send = call(split_body, [part, part], 0, 6, mib=60)(
        flat(source_fields),
        flat(receiver_fields),
        flat(courant),
        flat(epsilon),
        flat(delta_param),
        flat(tilt_angle),
    )
    got = sibling(send)
    edge12 = jax.ShapeDtypeStruct((6, ROWS, ZB, side), F32)
    edge8 = jax.ShapeDtypeStruct((4, ROWS, ZB, side), F32)
    merged = call(
        functools.partial(merge_body, sec_size),
        [jax.ShapeDtypeStruct((12, ROWS, ZB, side), F32)] + [edge12] * nz,
        0,
        2,
    )(keep, got)
    own, edges = merged[0], merged[1:]

    slots = receiver_data.shape[0]
    (inject,) = call(
        inject_body, [jax.ShapeDtypeStruct((slots, WROWS, WZ, side), F32)], 0, 2
    )(receiver_pos.T, receiver_data)

    def exchange(own, edges):
        sib_own, par_own = sibling(own), partner(own)
        halos = depth_halos(edges)
        groups = [(own, halos)]
        groups.append((sib_own, [sibling(h) for h in halos]))
        groups.append((par_own, [partner(h) for h in halos]))
        return groups

    snap_type = jax.ShapeDtypeStruct((SNAPS, ROWS, 2 * ZB, side), BF16)
    own_type = jax.ShapeDtypeStruct((8, ROWS, ZB, side), F32)
    fin_type = jax.ShapeDtypeStruct((8, ROWS, ZB, half), F32)

    coef_type = jax.ShapeDtypeStruct((5, WROWS, WZ, side), F32)

    def run_round(number, groups, coef, snaps, more, last):
        args = [step_counts, wavelet, source_pos]
        for own_, halos in groups:
            args += [own_] + list(halos)
        if number:
            args.append(coef)
        args.append(inject)
        if number:
            args.append(snaps)
        outs = [own_type, snap_type]
        if more:
            outs += [edge8] * nz
        if last:
            outs += [fin_type]
        if not number:
            outs += [coef_type]
        return call(
            functools.partial(round_body, number, sec_size, more, last),
            outs,
            3,
            len(args) - 3,
            [pltpu.VMEM((2, 2, WROWS, side // LANES, 2 * ZB + WZ, LANES), F32)] * 2,
            10000000,
            3000000,
            16,
            ROUND_FLAGS,
        )(*args)

    own, snaps, *rest = run_round(0, exchange(own, edges), None, None, True, False)
    edges, coef = rest[:nz], rest[nz]
    own, snaps, *rest = run_round(1, exchange(own, edges), coef, snaps, True, True)
    edges, final_send = rest[:nz], rest[nz]

    def third(own, snaps, final_send, *edges):
        return tuple(run_round(2, exchange(own, list(edges)), coef, snaps, False, True))

    def done(own, snaps, final_send, *edges):
        return own, snaps, final_send

    own, snaps, final_send = lax.cond(
        jnp.sum(step_counts) > 2 * HALO, third, done, own, snaps, final_send, *edges
    )
    final_got = sibling(final_send)
    sib = sibling(snaps)
    near, far = partner(snaps), partner(sib)
    sib_near, sib_far = sibling(near), sibling(far)
    n_lags = offset_lags.shape[0]
    out = jax.ShapeDtypeStruct((4 * depth_cells * wide_cells, half), F32)
    images, src, rec = call(
        image_body,
        [jax.ShapeDtypeStruct((n_lags, depth_cells, wide_cells, half), BF16), out, out],
        1,
        8,
        [
            pltpu.VMEM((SNAPS * 6 * ROWS, 2 * ZB, side), BF16),
            pltpu.VMEM((2 * LAG + 2, SNAPS * 6 * ROWS, 2 * ZB, half), F32),
            pltpu.VMEM((4, ZB * 2 * ROWS, half), F32),
        ],
        10000000,
        3000000,
        24,
    )(offset_lags.T, own, final_got, snaps, sib, near, far, sib_near, sib_far)
    shape = (4, depth_cells, wide_cells, half)
    return images, src.reshape(shape), rec.reshape(shape)


def solution(mesh):
    placed = (
        P("shot", "sec", "gx", "gy"),
        P("shot", "sec", "gx", "gy"),
        P("sec", "gx", "gy"),
        P("sec", "gx", "gy"),
        P("sec", "gx", "gy"),
        P("sec", "gx", "gy"),
        P("shot"),
        P("shot"),
        P("shot", None),
        P("shot", None),
        P(),
        P(),
    )
    return jax.shard_map(
        local,
        mesh=mesh,
        in_specs=placed,
        out_specs=(
            P("shot", "sec", "gx", "gy"),
            P("shot", "sec", "gx", "gy"),
            P("shot", "sec", "gx", "gy"),
        ),
        check_vma=False,
    )
```

```python
import functools

import jax
import jax.numpy as jnp
from jax import lax
from jax.experimental import pallas as pl
from jax.experimental.pallas import tpu as pltpu
from jax.sharding import PartitionSpec as P


SNAPS = 3
STEPS = 3
LAG = 8
HALO = 4
ROWS = 4
WROWS = ROWS + 2 * HALO
ZB = 8
WZ = ZB + 2 * HALO
LANES = 128

F32 = jnp.float32
BF16 = jnp.bfloat16
VM = pl.BlockSpec(memory_space=pltpu.VMEM)
SM = pl.BlockSpec(memory_space=pltpu.SMEM)


def call(body, outs, n_smem, n_vmem, scratch=(), flops=100000, moved=1000000, mib=12):
    return pl.pallas_call(
        body,
        out_shape=outs,
        in_specs=[SM] * n_smem + [VM] * n_vmem,
        out_specs=[VM] * len(outs),
        scratch_shapes=list(scratch),
        cost_estimate=pl.CostEstimate(flops=flops, bytes_accessed=moved, transcendentals=0),
        compiler_params=pltpu.CompilerParams(vmem_limit_bytes=mib * 2**20),
    )


def half_swap(value):
    return pltpu.roll(value, HALO, 0)


def low_sublanes(shape):
    return lax.broadcasted_iota(jnp.int32, shape, 0) < HALO


def edges_of(first, second, sec_size):
    sub = low_sublanes(first.shape)
    top = jnp.where(sub, half_swap(first), second)
    bottom = jnp.where(sub, first, half_swap(second))
    if sec_size == 2:
        return [jnp.where(lax.axis_index("sec") == 0, top, bottom)]
    return [top, bottom]


def split_body(sec_size, src, rec, courant, epsilon, delta, tilt, keep, send, *edges):
    low = lax.axis_index("gy") == 0
    nz = len(edges) // 2

    def pair(j, picks, change=lambda v: v):
        for r in range(ROWS):
            mine, other = [], []
            for k, pick in enumerate(picks):
                lo = pick(pl.ds(r, ZB, stride=2 * ROWS))
                hi = pick(pl.ds(r + ROWS, ZB, stride=2 * ROWS))
                if k == 1:
                    lo, hi = change(lo), change(hi)
                mine.append(jnp.where(low, lo, hi))
                other.append(jnp.where(low, hi, lo))
                keep[2 * j + k, r] = mine[k]
                send[2 * j + k, r] = other[k]
            for ref, edge in zip(edges[:nz], edges_of(*mine, sec_size)):
                ref[j, r] = edge
            for ref, edge in zip(edges[nz:], edges_of(*other, sec_size)):
                ref[j, r] = edge

    for j in range(2):
        pair(j, [lambda s, m=2 * j + k: src[m, s, :] for k in range(2)])
        pair(2 + j, [lambda s, m=2 * j + k: rec[m, s, :] for k in range(2)])
    pair(4, [lambda s: courant[s, :], lambda s: epsilon[s, :]])
    pair(5, [lambda s: delta[s, :], lambda s: tilt[s, :]], jnp.sin)


def copy_body(source, target):
    target[...] = source[...]


def merge_body(keep, got, own):
    low = lax.axis_index("gy") == 0
    half = keep.shape[-1]

    def one(n, _):
        for r in range(ROWS):
            a, b = keep[n, r], got[n, r]
            own[n, r, :, :half] = jnp.where(low, a, b)
            own[n, r, :, half:] = jnp.where(low, b, a)
        return 0

    lax.fori_loop(0, own.shape[0], one, 0)


def inject_body(pos_t, data, out):
    x0 = lax.axis_index("gx") * (2 * ROWS) + lax.axis_index("gy") * ROWS - HALO
    z0 = lax.axis_index("sec") * ZB - HALO
    count, side = pos_t.shape[1], out.shape[3]
    slots = out.shape[0]
    zw = pos_t[0:1, :] - z0
    xw = pos_t[1:2, :] - x0
    inside = (zw >= 0) & (zw < WZ) & (xw >= 0) & (xw < WROWS)
    cell = jnp.where(inside, xw * WZ + zw, -1)
    hit = lax.broadcasted_iota(jnp.int32, (WROWS * WZ, count), 0) == cell
    columns = lax.broadcasted_iota(jnp.int32, (side, count), 0)
    onehot = jnp.where(columns == pos_t[2:3, :], 1.0, 0.0).astype(BF16)

    for t in range(slots):
        amount = data[t : t + 1, :]
        first = amount.astype(BF16).astype(F32)
        rest = amount - first
        second = rest.astype(BF16).astype(F32)
        third = rest - second
        total = None
        for part in (first, second, third):
            left = jnp.where(hit, part, 0.0).astype(BF16)
            term = lax.dot_general(
                left, onehot, (((1,), (1,)), ((), ())), preferred_element_type=F32
            )
            total = term if total is None else total + term
        out[t] = total.reshape(WROWS, WZ, side)


def assemble(dest, j, base, own, halos, here, padded=False):
    sec = lax.axis_index("sec")
    zero = jnp.zeros(own.shape[2:], F32)
    has_low = here & (sec > 0)
    has_high = here & (sec < lax.axis_size("sec") - 1)
    for r in range(ROWS):
        sub = low_sublanes(own.shape[2:])
        below = jnp.where(has_low, halos[0][j, r], zero)
        above = jnp.where(has_high, halos[-1][j, r], zero)
        lows = (below, half_swap(below))
        highs = (half_swap(above), above)
        for k in range(2):
            mid = half_swap(jnp.where(here, own[2 * j + k, r], zero))
            ref = dest(k)
            upper = jnp.where(sub, lows[k], mid)
            lower = jnp.where(sub, mid, highs[k])
            if padded:
                for h in range(own.shape[3] // LANES):
                    lanes = slice(h * LANES, (h + 1) * LANES)
                    ref[base + r, h, ZB : 2 * ZB, :] = upper[:, lanes]
                    ref[base + r, h, 2 * ZB : 3 * ZB, :] = lower[:, lanes]
            else:
                ref[base + r, 0:ZB, :] = upper
                ref[base + r, ZB:WZ, :] = lower


def round_body(number, sec_size, more, last, *refs):
    refs = list(refs)

    def take(n):
        out = refs[:n]
        del refs[:n]
        return out

    opening = number == 0
    nz = 1 if sec_size == 2 else 2
    counts, wavelet, source_pos = take(3)
    groups = [(take(1)[0], take(nz)) for _ in range(3)]
    if not opening:
        coef = take(1)[0]
    inject = take(1)[0]
    snaps_in = None if opening else take(1)[0]
    own_out, snaps = take(2)
    edge_outs = take(nz) if more else []
    final_send = take(1)[0] if last else None
    if opening:
        coef = take(1)[0]
    works = take(2)

    low = lax.axis_index("gy") == 0
    gx = lax.axis_index("gx")
    sec = lax.axis_index("sec")
    zero = jnp.int32(0)
    always = gx >= 0
    has_partner = jnp.where(low, gx, lax.axis_size("gx") - 1 - gx) > 0
    bases = [
        (jnp.int32(HALO), always),
        (jnp.where(low, HALO + ROWS, 0), always),
        (jnp.where(low, 0, HALO + ROWS), has_partner),
    ]

    def fields(i, _):
        for parity in range(2):
            for (base, here), (own, halos) in zip(bases, groups):
                put_at = lambda k, work=works[parity]: work.at[i, k]
                assemble(put_at, 2 * i + parity, base, own, halos, here, True)
        return 0

    lax.fori_loop(0, 2, fields, 0)

    if opening:
        for j in range(2):
            for (base, here), (own, halos) in zip(bases, groups):
                assemble(lambda k: coef.at[2 * j + k], 4 + j, base, own, halos, here)

        def derive(x, _):
            c = coef[0, x]
            s = coef[3, x]
            wx = s * s
            coef[1, x] = c * (1.0 + 2.0 * coef[1, x])
            coef[2, x] = c * (1.0 + 2.0 * coef[2, x])
            coef[3, x] = wx
            coef[4, x] = 0.5 * s * jnp.sqrt(1.0 - wx)
            return 0

        lax.fori_loop(1, WROWS - 1, derive, 0)
    else:
        snaps[...] = snaps_in[...]

    ends = []
    total = zero
    for s in range(SNAPS):
        total = total + counts[s]
        ends.append(total)
    first = number * HALO
    todo = jnp.clip(total - first, 0, HALO)
    n_lane = works[0].shape[3]
    side = n_lane * LANES
    n_depth = WZ // ZB
    v_sub = lax.broadcasted_iota(jnp.int32, (ZB, LANES), 0)
    v_lane = lax.broadcasted_iota(jnp.int32, (ZB, LANES), 1)
    keys = [(t, h) for t in range(n_depth) for h in range(n_lane)]
    x0 = gx * (2 * ROWS) + lax.axis_index("gy") * ROWS - HALO
    sx = source_pos[1] - x0
    sz = source_pos[0] - (sec * ZB - HALO)
    sy = source_pos[2]

    def own_cells(parity, section, which, r):
        start = ZB + HALO
        parts = [
            works[parity][section, which, HALO + r, h, start : start + ZB, :]
            for h in range(n_lane)
        ]
        return jnp.concatenate(parts, axis=1)

    def tiles(ref, *at):
        return {
            (t, h): ref[at + (slice(t * ZB, (t + 1) * ZB), slice(h * LANES, (h + 1) * LANES))]
            for t, h in keys
        }

    def cells(parity, section, which, x, shift=0):
        start = ZB + shift
        return {
            (t, h): works[parity][section, which, x, h, start + t * ZB : start + (t + 1) * ZB, :]
            for t, h in keys
        }

    def side_sum(v):
        left = {k: pltpu.roll(v[k], 1, 1) for k in keys}
        right = {k: pltpu.roll(v[k], LANES - 1, 1) for k in keys}
        out = {}
        for t, h in keys:
            a = jnp.where(v_lane == 0, left.get((t, h - 1), 0.0), left[t, h])
            b = jnp.where(v_lane == LANES - 1, right.get((t, h + 1), 0.0), right[t, h])
            out[t, h] = a + b
        return out

    def put(value, parity, section, which, x):
        for t, h in keys:
            works[parity][section, which, x, h, (t + 1) * ZB : (t + 2) * ZB, :] = value[t, h]

    def step(j):
        active = first + j
        slot = zero
        start = zero
        for s in range(SNAPS):
            slot = jnp.where(active >= start, s * STEPS + active - start, slot)
            start = ends[s]
        cur = j % 2
        new = 1 - cur
        margin = todo - 1 - j

        def one_row(x, c, ce, cd, wx, wm, section):
            p, pm, pp = (cells(cur, section, 0, x + d) for d in (0, -1, 1))
            q, qm, qp = (cells(cur, section, 1, x + d) for d in (0, -1, 1))
            pu, pmu, ppu = (cells(cur, section, 0, x + d, 1) for d in (0, -1, 1))
            pd, pmd, ppd = (cells(cur, section, 0, x + d, -1) for d in (0, -1, 1))
            qu, qmu, qpu = (cells(cur, section, 1, x + d, 1) for d in (0, -1, 1))
            qd, qmd, qpd = (cells(cur, section, 1, x + d, -1) for d in (0, -1, 1))
            ys = side_sum(p)
            po = cells(new, section, 0, x)
            qo = cells(new, section, 1, x)
            extra = tiles(inject, slot, x) if section == 1 else None
            new_p, new_q = {}, {}
            for k in keys:
                zz = pu[k] + pd[k]
                xx = pp[k] + pm[k]
                xz = (ppu[k] - pmu[k]) - (ppd[k] - pmd[k])
                horiz = (xx + ys[k] - 4.0 * p[k]) + wx[k] * (zz - xx) - wm[k] * xz
                q2 = 2.0 * q[k]
                qz = qu[k] + qd[k]
                qx = qp[k] + qm[k]
                qxz = (qpu[k] - qmu[k]) - (qpd[k] - qmd[k])
                vert = c[k] * ((qz - q2) + wx[k] * (qx - qz) + wm[k] * qxz)
                new_p[k] = (2.0 * p[k] - po[k]) + (ce[k] * horiz + vert)
                new_q[k] = (q2 - qo[k]) + (cd[k] * horiz + vert)
                if extra is not None:
                    new_p[k] = new_p[k] + extra[k]
                    new_q[k] = new_q[k] + extra[k]
            put(new_p, new, section, 0, x)
            put(new_q, new, section, 1, x)

        def rows(i, _):
            for u in range(2):
                x = HALO - margin + 2 * i + u
                weights = [tiles(coef, n, x) for n in range(5)]
                for section in range(2):
                    one_row(x, *weights, section)
            return 0

        lax.fori_loop(0, ROWS // 2 + margin, rows, 0)

        @pl.when((sx >= 0) & (sx < WROWS))
        def _():
            amount = wavelet[slot]
            for t, h in keys:
                hit = (v_sub == sz - t * ZB) & (v_lane == sy - h * LANES)
                here = jnp.where(hit, amount, 0.0)
                for which in range(2):
                    at = (0, which, sx, h, slice((t + 1) * ZB, (t + 2) * ZB))
                    works[new][at] = works[new][at] + here

        for s in range(SNAPS):

            @pl.when(active + 1 == ends[s])
            def _():
                for r in range(ROWS):
                    both = [own_cells(new, section, 0, r) for section in range(2)]
                    snaps[s, r] = jnp.concatenate(both, axis=0).astype(BF16)

    for j in range(HALO):
        pl.when(j < todo)(functools.partial(step, j))

    odd = todo % 2 == 1
    for section in range(2):
        for old in range(2):
            for r in range(ROWS):
                both = []
                for which in range(2):
                    value = jnp.where(
                        odd,
                        own_cells(1 - old, section, which, r),
                        own_cells(old, section, which, r),
                    )
                    member = section * 4 + old * 2 + which
                    own_out[member, r] = value
                    if last:
                        final_send[member, r] = jnp.where(
                            low, value[:, side // 2 :], value[:, : side // 2]
                        )
                    both.append(value)
                if more:
                    for ref, edge in zip(edge_outs, edges_of(both[0], both[1], sec_size)):
                        ref[section * 2 + old, r] = edge


def fields_body(own, got, src, rec):
    low = lax.axis_index("gy") == 0
    half = got.shape[-1]
    mine = jnp.where(low, 0, ROWS)
    other = jnp.where(low, ROWS, 0)
    for member in range(8):
        dest = src if member < 4 else rec
        base = (member % 4) * ZB * 2 * ROWS
        for r in range(ROWS):
            value = own[member, r]
            value = jnp.where(low, value[:, :half], value[:, half:])
            dest[pl.ds(base + mine + r, ZB, stride=2 * ROWS), :] = value
            dest[pl.ds(base + other + r, ZB, stride=2 * ROWS), :] = got[member, r]


def image_body(lags, snaps, sib, near, far, sib_near, sib_far, images, rows, table, flip):
    core = lax.axis_index("gy")
    gx = lax.axis_index("gx")
    low = core == 0
    half = images.shape[3]
    side = rows.shape[-1]
    span = 6 * ROWS
    mine_on = jnp.where(low, gx, lax.axis_size("gx") - 1 - gx) > 0
    sib_on = jnp.where(low, lax.axis_size("gx") - 1 - gx, gx) > 0
    pieces = (
        (near, jnp.where(low, ROWS, 4 * ROWS), mine_on),
        (far, jnp.where(low, 0, 5 * ROWS), mine_on),
        (snaps, jnp.where(low, 2 * ROWS, 3 * ROWS), None),
        (sib, jnp.where(low, 3 * ROWS, 2 * ROWS), None),
        (sib_near, jnp.where(low, 4 * ROWS, ROWS), sib_on),
        (sib_far, jnp.where(low, 5 * ROWS, 0), sib_on),
    )
    for piece, base, here in pieces:
        for s in range(SNAPS):
            for r in range(ROWS):
                value = piece[s, r]
                if here is not None:
                    value = jnp.where(here, value, jnp.zeros_like(value))
                rows[s * span + base + r] = value

    cells = rows[...].reshape(SNAPS * span * 2 * ZB, side)
    lane = lax.broadcasted_iota(jnp.int32, (side, 2 * half), 1)
    second = (lane >= half).astype(jnp.int32)
    gap = lax.broadcasted_iota(jnp.int32, (side, 2 * half), 0) - core * half - lane + second * (half + 1)

    def shifts(i, _):
        for u in range(3):
            m = 3 * i + u
            pick = jnp.where(gap == LAG - 2 * m, 1.0, 0.0).astype(BF16)
            moved = jnp.dot(cells, pick, preferred_element_type=F32)
            for h in range(2):
                part = moved[:, h * half : (h + 1) * half]
                table[2 * m + h] = part.reshape(SNAPS * span, 2 * ZB, half)
        return 0

    lax.fori_loop(0, (LAG + 1) // 3, shifts, 0)

    count = lags.shape[1]
    group = next(g for g in (4, 3, 2, 1) if count % g == 0)

    def some_lags(i, _):
        for u in range(group):
            l = i * group + u
            lx = lags[0, l]
            ly = lags[1, l]
            total = None
            for s in range(SNAPS):
                at = s * span + 2 * ROWS
                a = table[LAG + ly, pl.ds(at - lx, 2 * ROWS), 0:ZB, :]
                b = table[LAG - ly, pl.ds(at + lx, 2 * ROWS), ZB : 2 * ZB, :]
                total = a * b if total is None else total + a * b
            for x in range(2 * ROWS):
                flip[u, pl.ds(x, ZB, stride=2 * ROWS), :] = total[x]
            images[l] = flip[u].reshape(ZB, 2 * ROWS, half).astype(BF16)
        return 0

    lax.fori_loop(0, count // group, some_lags, 0)


def local(
    source_fields,
    receiver_fields,
    courant,
    epsilon,
    delta_param,
    tilt_angle,
    source_pos,
    wavelet,
    receiver_pos,
    receiver_data,
    step_counts,
    offset_lags,
):
    sec_size = lax.axis_size("sec")
    gx_size = lax.axis_size("gx")
    depth_cells, wide_cells, half = courant.shape
    side = 2 * half
    shots, nz = lax.axis_size("shot"), (1 if sec_size == 2 else 2)
    axes = ("shot", "gx", "sec", "gy")

    def permute(x, move):
        def rank(d):
            return ((d[0] * gx_size + d[1]) * sec_size + d[2]) * 2 + d[3]

        pairs = [
            (rank((n, g, s, c)), rank(move(n, g, s, c)))
            for n in range(shots)
            for g in range(gx_size)
            for s in range(sec_size)
            for c in range(2)
        ]
        return lax.ppermute(x, axes, pairs)

    def sibling(x):
        return permute(x, lambda n, g, s, c: (n, g, s, 1 - c))

    def facing(n, g, s, c):
        other = g - 1 if c == 0 else g + 1
        if 0 <= other < gx_size:
            return (n, other, s, 1 - c)
        return ((n + 1) % shots, g, s, c)

    def abreast(n, g, s, c):
        other = g + 1 if c == 0 else g - 1
        if 0 <= other < gx_size:
            return (n, other, s, c)
        return (n, g, s, 1 - c)

    def partner(x):
        return permute(x, facing)

    def depth_halos(edges, flip=0):
        ups = [permute(edges[0], lambda n, g, s, c: (n, g, (s + 1) % sec_size, c ^ flip))]
        if nz == 2:
            ups.append(permute(edges[1], lambda n, g, s, c: (n, g, (s - 1) % sec_size, c ^ flip)))
        return ups

    def flat(x):
        return x.reshape(x.shape[:-3] + (depth_cells * wide_cells, half))

    part = jax.ShapeDtypeStruct((12, ROWS, ZB, half), F32)
    edge_part = jax.ShapeDtypeStruct((6, ROWS, ZB, half), F32)
    edge8 = jax.ShapeDtypeStruct((4, ROWS, ZB, side), F32)
    keep, send, *edges = call(
        functools.partial(split_body, sec_size), [part, part] + [edge_part] * (2 * nz), 0, 6, mib=60
    )(
        flat(source_fields),
        flat(receiver_fields),
        flat(courant),
        flat(epsilon),
        flat(delta_param),
        flat(tilt_angle),
    )

    def merge(a, b):
        out = jax.ShapeDtypeStruct(a.shape[:-1] + (side,), F32)
        return call(merge_body, [out], 0, 2)(a, b)[0]

    near_edges = depth_halos(edges[:nz])
    far_edges = depth_halos(edges[nz:], 1)
    par_keep = partner(keep)
    par_send = permute(send, abreast)
    got = sibling(send)
    sib_keep = sibling(keep)
    (keep,) = call(copy_body, [part], 0, 1)(keep)
    (send,) = call(copy_body, [part], 0, 1)(send)
    owns = [merge(keep, got), merge(send, sib_keep), merge(par_send, par_keep)]

    slots = receiver_data.shape[0]
    (inject,) = call(
        inject_body, [jax.ShapeDtypeStruct((slots, WROWS, WZ, side), F32)], 0, 2
    )(receiver_pos.T, receiver_data)

    def share(owns, halos):
        sib_halos = [sibling(h) for h in halos]
        par_halos = [partner(h) for h in halos]
        return list(zip(owns, (halos, sib_halos, par_halos)))

    def exchange(own, edges):
        return share([own, sibling(own), partner(own)], depth_halos(edges))

    snap_type = jax.ShapeDtypeStruct((SNAPS, ROWS, 2 * ZB, side), BF16)
    own_type = jax.ShapeDtypeStruct((8, ROWS, ZB, side), F32)
    fin_type = jax.ShapeDtypeStruct((8, ROWS, ZB, half), F32)

    coef_type = jax.ShapeDtypeStruct((5, WROWS, WZ, side), F32)

    def run_round(number, groups, coef, snaps, more, last):
        args = [step_counts, wavelet, source_pos]
        for own_, halos in groups:
            args += [own_] + list(halos)
        if number:
            args.append(coef)
        args.append(inject)
        if number:
            args.append(snaps)
        outs = [own_type, snap_type]
        if more:
            outs += [edge8] * nz
        if last:
            outs += [fin_type]
        if not number:
            outs += [coef_type]
        return call(
            functools.partial(round_body, number, sec_size, more, last),
            outs,
            3,
            len(args) - 3,
            [pltpu.VMEM((2, 2, WROWS, side // LANES, 2 * ZB + WZ, LANES), F32)] * 2,
            10000000,
            3000000,
            16,
        )(*args)

    halos = [merge(a, b) for a, b in zip(near_edges, far_edges)]
    groups = share(owns, halos)
    own, snaps, *rest = run_round(0, groups, None, None, True, False)
    edges, coef = rest[:nz], rest[nz]
    own, snaps, *rest = run_round(1, exchange(own, edges), coef, snaps, True, True)
    edges, final_send = rest[:nz], rest[nz]

    def third(own, snaps, final_send, *edges):
        return tuple(run_round(2, exchange(own, list(edges)), coef, snaps, False, True))

    def done(own, snaps, final_send, *edges):
        return own, snaps, final_send

    own, snaps, final_send = lax.cond(
        jnp.sum(step_counts) > 2 * HALO, third, done, own, snaps, final_send, *edges
    )
    final_got = sibling(final_send)
    sib = sibling(snaps)
    near, far = partner(snaps), partner(sib)
    sib_near, sib_far = sibling(near), sibling(far)
    n_lags = offset_lags.shape[0]
    out = jax.ShapeDtypeStruct((4 * depth_cells * wide_cells, half), F32)
    src, rec = call(fields_body, [out, out], 0, 2)(own, final_got)
    (images,) = call(
        image_body,
        [jax.ShapeDtypeStruct((n_lags, depth_cells, wide_cells, half), BF16)],
        1,
        6,
        [
            pltpu.VMEM((SNAPS * 6 * ROWS, 2 * ZB, side), BF16),
            pltpu.VMEM((2 * LAG + 2, SNAPS * 6 * ROWS, 2 * ZB, half), F32),
            pltpu.VMEM((4, ZB * 2 * ROWS, half), F32),
        ],
        10000000,
        3000000,
        24,
    )(offset_lags.T, snaps, sib, near, far, sib_near, sib_far)
    shape = (4, depth_cells, wide_cells, half)
    return images, src.reshape(shape), rec.reshape(shape)


def solution(mesh):
    placed = (
        P("shot", "sec", "gx", "gy"),
        P("shot", "sec", "gx", "gy"),
        P("sec", "gx", "gy"),
        P("sec", "gx", "gy"),
        P("sec", "gx", "gy"),
        P("sec", "gx", "gy"),
        P("shot"),
        P("shot"),
        P("shot", None),
        P("shot", None),
        P(),
        P(),
    )
    return jax.shard_map(
        local,
        mesh=mesh,
        in_specs=placed,
        out_specs=(
            P("shot", "sec", "gx", "gy"),
            P("shot", "sec", "gx", "gy"),
            P("shot", "sec", "gx", "gy"),
        ),
        check_vma=False,
    )
```

```python
import functools

import jax
import jax.numpy as jnp
from jax import lax
from jax.experimental import pallas as pl
from jax.experimental.pallas import tpu as pltpu
from jax.sharding import PartitionSpec as P


SNAPS = 3
STEPS = 3
LAG = 8
HALO = 4
ROWS = 4
WROWS = ROWS + 2 * HALO
ZB = 8
WZ = ZB + 2 * HALO
LANES = 128

F32 = jnp.float32
BF16 = jnp.bfloat16
VM = pl.BlockSpec(memory_space=pltpu.VMEM)
SM = pl.BlockSpec(memory_space=pltpu.SMEM)


def call(body, outs, n_smem, n_vmem, scratch=(), flops=100000, moved=1000000, mib=12):
    return pl.pallas_call(
        body,
        out_shape=outs,
        in_specs=[SM] * n_smem + [VM] * n_vmem,
        out_specs=[VM] * len(outs),
        scratch_shapes=list(scratch),
        cost_estimate=pl.CostEstimate(flops=flops, bytes_accessed=moved, transcendentals=0),
        compiler_params=pltpu.CompilerParams(vmem_limit_bytes=mib * 2**20),
    )


def half_swap(value):
    return pltpu.roll(value, HALO, 0)


def low_sublanes(shape):
    return lax.broadcasted_iota(jnp.int32, shape, 0) < HALO


def edges_of(first, second, sec_size):
    sub = low_sublanes(first.shape)
    top = jnp.where(sub, half_swap(first), second)
    bottom = jnp.where(sub, first, half_swap(second))
    if sec_size == 2:
        return [jnp.where(lax.axis_index("sec") == 0, top, bottom)]
    return [top, bottom]


def split_body(sec_size, src, rec, courant, epsilon, delta, tilt, keep, send, *edges):
    low = lax.axis_index("gy") == 0
    nz = len(edges) // 2

    def pair(j, picks, change=lambda v: v):
        for r in range(ROWS):
            mine, other = [], []
            for k, pick in enumerate(picks):
                lo = pick(pl.ds(r, ZB, stride=2 * ROWS))
                hi = pick(pl.ds(r + ROWS, ZB, stride=2 * ROWS))
                if k == 1:
                    lo, hi = change(lo), change(hi)
                mine.append(jnp.where(low, lo, hi))
                other.append(jnp.where(low, hi, lo))
                keep[2 * j + k, r] = mine[k]
                send[2 * j + k, r] = other[k]
            for ref, edge in zip(edges[:nz], edges_of(*mine, sec_size)):
                ref[j, r] = edge
            for ref, edge in zip(edges[nz:], edges_of(*other, sec_size)):
                ref[j, r] = edge

    for j in range(2):
        pair(j, [lambda s, m=2 * j + k: src[m, s, :] for k in range(2)])
        pair(2 + j, [lambda s, m=2 * j + k: rec[m, s, :] for k in range(2)])
    pair(4, [lambda s: courant[s, :], lambda s: epsilon[s, :]])
    pair(5, [lambda s: delta[s, :], lambda s: tilt[s, :]], jnp.sin)


def copy_body(source, target):
    target[...] = source[...]


def merge_body(keep, got, own):
    low = lax.axis_index("gy") == 0
    half = keep.shape[-1]

    def one(n, _):
        for r in range(ROWS):
            a, b = keep[n, r], got[n, r]
            own[n, r, :, :half] = jnp.where(low, a, b)
            own[n, r, :, half:] = jnp.where(low, b, a)
        return 0

    lax.fori_loop(0, own.shape[0], one, 0)


def inject_body(pos_t, data, out):
    x0 = lax.axis_index("gx") * (2 * ROWS) + lax.axis_index("gy") * ROWS - HALO
    z0 = lax.axis_index("sec") * ZB - HALO
    count, side = pos_t.shape[1], out.shape[3]
    slots = out.shape[0]
    zw = pos_t[0:1, :] - z0
    xw = pos_t[1:2, :] - x0
    inside = (zw >= 0) & (zw < WZ) & (xw >= 0) & (xw < WROWS)
    cell = jnp.where(inside, xw * WZ + zw, -1)
    hit = lax.broadcasted_iota(jnp.int32, (WROWS * WZ, count), 0) == cell
    columns = lax.broadcasted_iota(jnp.int32, (side, count), 0)
    onehot = jnp.where(columns == pos_t[2:3, :], 1.0, 0.0).astype(BF16)

    for t in range(slots):
        amount = data[t : t + 1, :]
        first = amount.astype(BF16).astype(F32)
        rest = amount - first
        second = rest.astype(BF16).astype(F32)
        third = rest - second
        total = None
        for part in (first, second, third):
            left = jnp.where(hit, part, 0.0).astype(BF16)
            term = lax.dot_general(
                left, onehot, (((1,), (1,)), ((), ())), preferred_element_type=F32
            )
            total = term if total is None else total + term
        out[t] = total.reshape(WROWS, WZ, side)


def assemble(dest, j, base, own, halos, here, padded=False):
    sec = lax.axis_index("sec")
    zero = jnp.zeros(own.shape[2:], F32)
    has_low = here & (sec > 0)
    has_high = here & (sec < lax.axis_size("sec") - 1)
    for r in range(ROWS):
        sub = low_sublanes(own.shape[2:])
        below = jnp.where(has_low, halos[0][j, r], zero)
        above = jnp.where(has_high, halos[-1][j, r], zero)
        lows = (below, half_swap(below))
        highs = (half_swap(above), above)
        for k in range(2):
            mid = half_swap(jnp.where(here, own[2 * j + k, r], zero))
            ref = dest(k)
            upper = jnp.where(sub, lows[k], mid)
            lower = jnp.where(sub, mid, highs[k])
            if padded:
                for h in range(own.shape[3] // LANES):
                    lanes = slice(h * LANES, (h + 1) * LANES)
                    ref[base + r, h, ZB : 2 * ZB, :] = upper[:, lanes]
                    ref[base + r, h, 2 * ZB : 3 * ZB, :] = lower[:, lanes]
            else:
                ref[base + r, 0:ZB, :] = upper
                ref[base + r, ZB:WZ, :] = lower


def round_body(number, sec_size, more, last, *refs):
    refs = list(refs)

    def take(n):
        out = refs[:n]
        del refs[:n]
        return out

    opening = number == 0
    nz = 1 if sec_size == 2 else 2
    counts, wavelet, source_pos = take(3)
    groups = [(take(1)[0], take(nz)) for _ in range(3)]
    if not opening:
        coef = take(1)[0]
    inject = take(1)[0]
    snaps_in = None if opening else take(1)[0]
    own_out, snaps = take(2)
    edge_outs = take(nz) if more else []
    final_send = take(1)[0] if last else None
    if opening:
        coef = take(1)[0]
    works = take(2)

    low = lax.axis_index("gy") == 0
    gx = lax.axis_index("gx")
    sec = lax.axis_index("sec")
    zero = jnp.int32(0)
    always = gx >= 0
    has_partner = jnp.where(low, gx, lax.axis_size("gx") - 1 - gx) > 0
    bases = [
        (jnp.int32(HALO), always),
        (jnp.where(low, HALO + ROWS, 0), always),
        (jnp.where(low, 0, HALO + ROWS), has_partner),
    ]

    def fields(i, _):
        for parity in range(2):
            for (base, here), (own, halos) in zip(bases, groups):
                put_at = lambda k, work=works[parity]: work.at[i, k]
                assemble(put_at, 2 * i + parity, base, own, halos, here, True)
        return 0

    lax.fori_loop(0, 2, fields, 0)

    if opening:
        for j in range(2):
            for (base, here), (own, halos) in zip(bases, groups):
                assemble(lambda k: coef.at[2 * j + k], 4 + j, base, own, halos, here)

        def derive(x, _):
            c = coef[0, x]
            s = coef[3, x]
            wx = s * s
            coef[1, x] = c * (1.0 + 2.0 * coef[1, x])
            coef[2, x] = c * (1.0 + 2.0 * coef[2, x])
            coef[3, x] = wx
            coef[4, x] = 0.5 * s * jnp.sqrt(1.0 - wx)
            return 0

        lax.fori_loop(1, WROWS - 1, derive, 0)
    else:
        snaps[...] = snaps_in[...]

    ends = []
    total = zero
    for s in range(SNAPS):
        total = total + counts[s]
        ends.append(total)
    first = number * HALO
    todo = jnp.clip(total - first, 0, HALO)
    n_lane = works[0].shape[3]
    side = n_lane * LANES
    n_depth = WZ // ZB
    v_sub = lax.broadcasted_iota(jnp.int32, (ZB, LANES), 0)
    v_lane = lax.broadcasted_iota(jnp.int32, (ZB, LANES), 1)
    keys = [(t, h) for t in range(n_depth) for h in range(n_lane)]
    x0 = gx * (2 * ROWS) + lax.axis_index("gy") * ROWS - HALO
    sx = source_pos[1] - x0
    sz = source_pos[0] - (sec * ZB - HALO)
    sy = source_pos[2]

    def own_cells(parity, section, which, r):
        start = ZB + HALO
        parts = [
            works[parity][section, which, HALO + r, h, start : start + ZB, :]
            for h in range(n_lane)
        ]
        return jnp.concatenate(parts, axis=1)

    def tiles(ref, *at):
        return {
            (t, h): ref[at + (slice(t * ZB, (t + 1) * ZB), slice(h * LANES, (h + 1) * LANES))]
            for t, h in keys
        }

    def cells(parity, section, which, x, shift=0):
        start = ZB + shift
        return {
            (t, h): works[parity][section, which, x, h, start + t * ZB : start + (t + 1) * ZB, :]
            for t, h in keys
        }

    def side_sum(v):
        left = {k: pltpu.roll(v[k], 1, 1) for k in keys}
        right = {k: pltpu.roll(v[k], LANES - 1, 1) for k in keys}
        out = {}
        for t, h in keys:
            a = jnp.where(v_lane == 0, left.get((t, h - 1), 0.0), left[t, h])
            b = jnp.where(v_lane == LANES - 1, right.get((t, h + 1), 0.0), right[t, h])
            out[t, h] = a + b
        return out

    def put(value, parity, section, which, x):
        for t, h in keys:
            works[parity][section, which, x, h, (t + 1) * ZB : (t + 2) * ZB, :] = value[t, h]

    def step(j):
        active = first + j
        slot = zero
        start = zero
        for s in range(SNAPS):
            slot = jnp.where(active >= start, s * STEPS + active - start, slot)
            start = ends[s]
        cur = j % 2
        new = 1 - cur
        margin = todo - 1 - j

        def one_row(x, c, ce, cd, wx, wm, section):
            p, pm, pp = (cells(cur, section, 0, x + d) for d in (0, -1, 1))
            q, qm, qp = (cells(cur, section, 1, x + d) for d in (0, -1, 1))
            pu, pmu, ppu = (cells(cur, section, 0, x + d, 1) for d in (0, -1, 1))
            pd, pmd, ppd = (cells(cur, section, 0, x + d, -1) for d in (0, -1, 1))
            qu, qmu, qpu = (cells(cur, section, 1, x + d, 1) for d in (0, -1, 1))
            qd, qmd, qpd = (cells(cur, section, 1, x + d, -1) for d in (0, -1, 1))
            ys = side_sum(p)
            po = cells(new, section, 0, x)
            qo = cells(new, section, 1, x)
            extra = tiles(inject, slot, x) if section == 1 else None
            new_p, new_q = {}, {}
            for k in keys:
                zz = pu[k] + pd[k]
                xx = pp[k] + pm[k]
                xz = (ppu[k] - pmu[k]) - (ppd[k] - pmd[k])
                horiz = (xx + ys[k] - 4.0 * p[k]) + wx[k] * (zz - xx) - wm[k] * xz
                q2 = 2.0 * q[k]
                qz = qu[k] + qd[k]
                qx = qp[k] + qm[k]
                qxz = (qpu[k] - qmu[k]) - (qpd[k] - qmd[k])
                vert = c[k] * ((qz - q2) + wx[k] * (qx - qz) + wm[k] * qxz)
                new_p[k] = (2.0 * p[k] - po[k]) + (ce[k] * horiz + vert)
                new_q[k] = (q2 - qo[k]) + (cd[k] * horiz + vert)
                if extra is not None:
                    new_p[k] = new_p[k] + extra[k]
                    new_q[k] = new_q[k] + extra[k]
            put(new_p, new, section, 0, x)
            put(new_q, new, section, 1, x)

        def rows(i, _):
            for u in range(2):
                x = HALO - margin + 2 * i + u
                weights = [tiles(coef, n, x) for n in range(5)]
                for section in range(2):
                    one_row(x, *weights, section)
            return 0

        lax.fori_loop(0, ROWS // 2 + margin, rows, 0)

        @pl.when((sx >= 0) & (sx < WROWS))
        def _():
            amount = wavelet[slot]
            for t, h in keys:
                hit = (v_sub == sz - t * ZB) & (v_lane == sy - h * LANES)
                here = jnp.where(hit, amount, 0.0)
                for which in range(2):
                    at = (0, which, sx, h, slice((t + 1) * ZB, (t + 2) * ZB))
                    works[new][at] = works[new][at] + here

        for s in range(SNAPS):

            @pl.when(active + 1 == ends[s])
            def _():
                for r in range(ROWS):
                    both = [own_cells(new, section, 0, r) for section in range(2)]
                    snaps[s, r] = jnp.concatenate(both, axis=0).astype(BF16)

    for j in range(HALO):
        pl.when(j < todo)(functools.partial(step, j))

    odd = todo % 2 == 1
    for section in range(2):
        for old in range(2):
            for r in range(ROWS):
                both = []
                for which in range(2):
                    value = jnp.where(
                        odd,
                        own_cells(1 - old, section, which, r),
                        own_cells(old, section, which, r),
                    )
                    member = section * 4 + old * 2 + which
                    own_out[member, r] = value
                    if last:
                        final_send[member, r] = jnp.where(
                            low, value[:, side // 2 :], value[:, : side // 2]
                        )
                    both.append(value)
                if more:
                    for ref, edge in zip(edge_outs, edges_of(both[0], both[1], sec_size)):
                        ref[section * 2 + old, r] = edge


def fields_body(own, got, src, rec):
    low = lax.axis_index("gy") == 0
    half = got.shape[-1]
    mine = jnp.where(low, 0, ROWS)
    other = jnp.where(low, ROWS, 0)
    for member in range(8):
        dest = src if member < 4 else rec
        base = (member % 4) * ZB * 2 * ROWS
        for r in range(ROWS):
            value = own[member, r]
            value = jnp.where(low, value[:, :half], value[:, half:])
            dest[pl.ds(base + mine + r, ZB, stride=2 * ROWS), :] = value
            dest[pl.ds(base + other + r, ZB, stride=2 * ROWS), :] = got[member, r]


def image_body(lags, snaps, sib, near, far, sib_near, sib_far, images, rows, table, flip):
    core = lax.axis_index("gy")
    gx = lax.axis_index("gx")
    low = core == 0
    half = images.shape[3]
    side = rows.shape[-1]
    span = 6 * ROWS
    mine_on = jnp.where(low, gx, lax.axis_size("gx") - 1 - gx) > 0
    sib_on = jnp.where(low, lax.axis_size("gx") - 1 - gx, gx) > 0
    pieces = (
        (near, jnp.where(low, ROWS, 4 * ROWS), mine_on),
        (far, jnp.where(low, 0, 5 * ROWS), mine_on),
        (snaps, jnp.where(low, 2 * ROWS, 3 * ROWS), None),
        (sib, jnp.where(low, 3 * ROWS, 2 * ROWS), None),
        (sib_near, jnp.where(low, 4 * ROWS, ROWS), sib_on),
        (sib_far, jnp.where(low, 5 * ROWS, 0), sib_on),
    )
    for piece, base, here in pieces:
        for s in range(SNAPS):
            for r in range(ROWS):
                value = piece[s, r]
                if here is not None:
                    value = jnp.where(here, value, jnp.zeros_like(value))
                rows[s * span + base + r] = value
                middle = value.astype(F32)
                table[LAG, s * span + base + r] = jnp.where(low, middle[:, :half], middle[:, half:])

    cells = rows[...].reshape(SNAPS * span * 2 * ZB, side)
    lane = lax.broadcasted_iota(jnp.int32, (side, 2 * half), 1)
    second = (lane >= half).astype(jnp.int32)
    gap = lax.broadcasted_iota(jnp.int32, (side, 2 * half), 0) - core * half - lane + second * (half + 1)

    def shifts(i, _):
        for first in (0, LAG + 1):
            for u in range(2):
                at = first + 4 * i + 2 * u
                pick = jnp.where(gap == LAG - at, 1.0, 0.0).astype(BF16)
                moved = jnp.dot(cells, pick, preferred_element_type=F32)
                for h in range(2):
                    part = moved[:, h * half : (h + 1) * half]
                    table[at + h] = part.reshape(SNAPS * span, 2 * ZB, half)
        return 0

    lax.fori_loop(0, LAG // 4, shifts, 0)

    count = lags.shape[1]
    group = next(g for g in (4, 3, 2, 1) if count % g == 0)

    def some_lags(i, _):
        for u in range(group):
            l = i * group + u
            lx = lags[0, l]
            ly = lags[1, l]
            total = None
            for s in range(SNAPS):
                at = s * span + 2 * ROWS
                a = table[LAG + ly, pl.ds(at - lx, 2 * ROWS), 0:ZB, :]
                b = table[LAG - ly, pl.ds(at + lx, 2 * ROWS), ZB : 2 * ZB, :]
                total = a * b if total is None else total + a * b
            for x in range(2 * ROWS):
                flip[u, pl.ds(x, ZB, stride=2 * ROWS), :] = total[x]
            images[l] = flip[u].reshape(ZB, 2 * ROWS, half).astype(BF16)
        return 0

    lax.fori_loop(0, count // group, some_lags, 0)


def local(
    source_fields,
    receiver_fields,
    courant,
    epsilon,
    delta_param,
    tilt_angle,
    source_pos,
    wavelet,
    receiver_pos,
    receiver_data,
    step_counts,
    offset_lags,
):
    sec_size = lax.axis_size("sec")
    gx_size = lax.axis_size("gx")
    depth_cells, wide_cells, half = courant.shape
    side = 2 * half
    shots, nz = lax.axis_size("shot"), (1 if sec_size == 2 else 2)
    axes = ("shot", "gx", "sec", "gy")

    def permute(x, move):
        def rank(d):
            return ((d[0] * gx_size + d[1]) * sec_size + d[2]) * 2 + d[3]

        pairs = [
            (rank((n, g, s, c)), rank(move(n, g, s, c)))
            for n in range(shots)
            for g in range(gx_size)
            for s in range(sec_size)
            for c in range(2)
        ]
        return lax.ppermute(x, axes, pairs)

    def sibling(x):
        return permute(x, lambda n, g, s, c: (n, g, s, 1 - c))

    def facing(n, g, s, c):
        other = g - 1 if c == 0 else g + 1
        if 0 <= other < gx_size:
            return (n, other, s, 1 - c)
        return ((n + 1) % shots, g, s, c)

    def abreast(n, g, s, c):
        other = g + 1 if c == 0 else g - 1
        if 0 <= other < gx_size:
            return (n, other, s, c)
        return (n, g, s, 1 - c)

    def partner(x):
        return permute(x, facing)

    def depth_halos(edges, flip=0):
        ups = [permute(edges[0], lambda n, g, s, c: (n, g, (s + 1) % sec_size, c ^ flip))]
        if nz == 2:
            ups.append(permute(edges[1], lambda n, g, s, c: (n, g, (s - 1) % sec_size, c ^ flip)))
        return ups

    def flat(x):
        return x.reshape(x.shape[:-3] + (depth_cells * wide_cells, half))

    part = jax.ShapeDtypeStruct((12, ROWS, ZB, half), F32)
    edge_part = jax.ShapeDtypeStruct((6, ROWS, ZB, half), F32)
    edge8 = jax.ShapeDtypeStruct((4, ROWS, ZB, side), F32)
    keep, send, *edges = call(
        functools.partial(split_body, sec_size), [part, part] + [edge_part] * (2 * nz), 0, 6, mib=60
    )(
        flat(source_fields),
        flat(receiver_fields),
        flat(courant),
        flat(epsilon),
        flat(delta_param),
        flat(tilt_angle),
    )

    def merge(a, b):
        out = jax.ShapeDtypeStruct(a.shape[:-1] + (side,), F32)
        return call(merge_body, [out], 0, 2)(a, b)[0]

    near_edges = depth_halos(edges[:nz])
    far_edges = depth_halos(edges[nz:], 1)
    par_keep = partner(keep)
    par_send = permute(send, abreast)
    got = sibling(send)
    sib_keep = sibling(keep)
    (keep,) = call(copy_body, [part], 0, 1)(keep)
    (send,) = call(copy_body, [part], 0, 1)(send)
    owns = [merge(keep, got), merge(send, sib_keep), merge(par_send, par_keep)]

    slots = receiver_data.shape[0]
    (inject,) = call(
        inject_body, [jax.ShapeDtypeStruct((slots, WROWS, WZ, side), F32)], 0, 2
    )(receiver_pos.T, receiver_data)

    def share(owns, halos):
        sib_halos = [sibling(h) for h in halos]
        par_halos = [partner(h) for h in halos]
        return list(zip(owns, (halos, sib_halos, par_halos)))

    def exchange(own, edges):
        return share([own, sibling(own), partner(own)], depth_halos(edges))

    snap_type = jax.ShapeDtypeStruct((SNAPS, ROWS, 2 * ZB, side), BF16)
    own_type = jax.ShapeDtypeStruct((8, ROWS, ZB, side), F32)
    fin_type = jax.ShapeDtypeStruct((8, ROWS, ZB, half), F32)

    coef_type = jax.ShapeDtypeStruct((5, WROWS, WZ, side), F32)

    def run_round(number, groups, coef, snaps, more, last):
        args = [step_counts, wavelet, source_pos]
        for own_, halos in groups:
            args += [own_] + list(halos)
        if number:
            args.append(coef)
        args.append(inject)
        if number:
            args.append(snaps)
        outs = [own_type, snap_type]
        if more:
            outs += [edge8] * nz
        if last:
            outs += [fin_type]
        if not number:
            outs += [coef_type]
        return call(
            functools.partial(round_body, number, sec_size, more, last),
            outs,
            3,
            len(args) - 3,
            [pltpu.VMEM((2, 2, WROWS, side // LANES, 2 * ZB + WZ, LANES), F32)] * 2,
            10000000,
            3000000,
            16,
        )(*args)

    halos = [merge(a, b) for a, b in zip(near_edges, far_edges)]
    groups = share(owns, halos)
    own, snaps, *rest = run_round(0, groups, None, None, True, False)
    edges, coef = rest[:nz], rest[nz]
    own, snaps, *rest = run_round(1, exchange(own, edges), coef, snaps, True, True)
    edges, final_send = rest[:nz], rest[nz]

    def third(own, snaps, final_send, *edges):
        return tuple(run_round(2, exchange(own, list(edges)), coef, snaps, False, True))

    def done(own, snaps, final_send, *edges):
        return own, snaps, final_send

    own, snaps, final_send = lax.cond(
        jnp.sum(step_counts) > 2 * HALO, third, done, own, snaps, final_send, *edges
    )
    final_got = sibling(final_send)
    sib = sibling(snaps)
    near, far = partner(snaps), partner(sib)
    sib_near, sib_far = sibling(near), sibling(far)
    n_lags = offset_lags.shape[0]
    out = jax.ShapeDtypeStruct((4 * depth_cells * wide_cells, half), F32)
    src, rec = call(fields_body, [out, out], 0, 2)(own, final_got)
    (images,) = call(
        image_body,
        [jax.ShapeDtypeStruct((n_lags, depth_cells, wide_cells, half), BF16)],
        1,
        6,
        [
            pltpu.VMEM((SNAPS * 6 * ROWS, 2 * ZB, side), BF16),
            pltpu.VMEM((2 * LAG + 1, SNAPS * 6 * ROWS, 2 * ZB, half), F32),
            pltpu.VMEM((4, ZB * 2 * ROWS, half), F32),
        ],
        10000000,
        3000000,
        24,
    )(offset_lags.T, snaps, sib, near, far, sib_near, sib_far)
    shape = (4, depth_cells, wide_cells, half)
    return images, src.reshape(shape), rec.reshape(shape)


def solution(mesh):
    placed = (
        P("shot", "sec", "gx", "gy"),
        P("shot", "sec", "gx", "gy"),
        P("sec", "gx", "gy"),
        P("sec", "gx", "gy"),
        P("sec", "gx", "gy"),
        P("sec", "gx", "gy"),
        P("shot"),
        P("shot"),
        P("shot", None),
        P("shot", None),
        P(),
        P(),
    )
    return jax.shard_map(
        local,
        mesh=mesh,
        in_specs=placed,
        out_specs=(
            P("shot", "sec", "gx", "gy"),
            P("shot", "sec", "gx", "gy"),
            P("shot", "sec", "gx", "gy"),
        ),
        check_vma=False,
    )
```
